32 devices in a mesh: gy: 4 (over y, x), gx: 8 (over z, core).
Axes of the slice: x: 2, y: 2, z: 4, core: 2. Of those that a mesh axis runs over, the one named last changes fastest.
Arguments:
- cost_volume: int32 [64, 128, 256], P('gy', 'gx'), may hold values from 0 to 64
- left_image: float32 [64, 128], P('gy', 'gx'), may hold values from -6 to 6
- p_small: int32 [4], replicated, may hold values from 4 to 16
- p_large: int32 [4], replicated, may hold values from 32 to 128
Outputs:
- aggregated: float32 [64, 128, 256], P('gy', 'gx')
The draws below stay inside these ranges and needn't reach their ends.
Inputs may be any that keep to these rules, and one draw needn't show every extreme that they name: `p_small`: every small penalty is below every large penalty.
All inputs are finite; a program needn't handle non-finite values.
Results may differ from the reference program's by a relative error of at most 0.00002.
Values sent between devices are 32-bit elements; how exact they have to be, the bound alone decides.
A program may use at most 64 MiB of HBM per device.

```python
from functools import partial
import jax
import jax.numpy as jnp
from jax import lax

DSP = 256
H = 64
W = 128


def draw_cost_volume(key, part):
    subkeys = jax.random.split(jax.random.fold_in(key, 11), 10)
    row_index = jnp.arange(H, dtype=jnp.int32)[:, None]
    column_index = jnp.arange(W, dtype=jnp.int32)[None, :]
    stripe_span = jax.random.randint(subkeys[0], (), W * 3 // 8, W // 2 + 1, dtype=jnp.int32)
    stripe_start = jax.random.randint(subkeys[1], (), W // 8, W - stripe_span - W // 8 + 1, dtype=jnp.int32)
    band_span = jax.random.randint(subkeys[2], (), H * 3 // 8, H // 2 + 1, dtype=jnp.int32)
    band_start = jax.random.randint(subkeys[3], (), H // 8, H - band_span - H // 8 + 1, dtype=jnp.int32)
    in_stripe = jnp.logical_and(column_index >= stripe_start, column_index < stripe_start + stripe_span)
    in_band = jnp.logical_and(row_index >= band_start, row_index < band_start + band_span)
    untextured = jnp.logical_or(in_stripe, in_band)
    slope_cols = jax.random.randint(subkeys[4], (), -(DSP // 2), DSP // 2 + 1, dtype=jnp.int32)
    slope_rows = jax.random.randint(subkeys[5], (), -(DSP // 2), DSP // 2 + 1, dtype=jnp.int32)
    shift_base = jax.random.randint(subkeys[6], (), 0, DSP, dtype=jnp.int32)
    jitter = jax.random.randint(subkeys[7], (H, W), -1, 2, dtype=jnp.int32)
    surface = jnp.mod(shift_base + slope_cols * column_index // W + slope_rows * row_index // H + jitter, DSP)
    labels = jnp.arange(DSP, dtype=jnp.int32)
    distance = jnp.minimum(jnp.abs(labels[None, None, :] - surface[:, :, None]), 10)
    textured = jnp.minimum(jax.random.randint(subkeys[8], (H, W, DSP), 0, 25, dtype=jnp.int32) + 4 * distance, 64)
    plateau = jax.random.randint(subkeys[9], (H, W), 8, 57, dtype=jnp.int32)
    return jnp.where(untextured[:, :, None], plateau[:, :, None], textured).astype(jnp.int32)


def with_ends(drawn, key, smallest, largest):
    shape = drawn.shape
    place = [jax.random.randint(jax.random.fold_in(key, axis), (), 0, shape[axis]) for axis in range(len(shape))]
    drawn = drawn.at[tuple(place)].set(smallest)
    longest = shape.index(max(shape))
    place[longest] = (place[longest] + 1) % shape[longest]
    return drawn.at[tuple(place)].set(largest)


def steps_of(own_key, extent, cuts, least, top_value):
    gain, own = 1.0, jax.random.fold_in(own_key, 6)
    for axis_at, parts in cuts:
        steps = jnp.exp(jax.random.uniform(jax.random.fold_in(own, axis_at), (parts,), jnp.float32, least / len(cuts), top_value / len(cuts)))
        gain = gain * jnp.repeat(steps, extent[axis_at] // parts).reshape([-1 if axis == axis_at else 1 for axis in range(len(extent))])
    return gain


def gaussian(own_key, dims, spread, limit, shards=(), kind=jnp.bfloat16):
    gain = steps_of(own_key, dims, shards, -0.22, 0.18) if shards else 1.0
    array = jax.random.normal(own_key, dims, jnp.float32) * spread * gain
    return jnp.minimum(jnp.maximum(array, -limit), limit).astype(kind)


def setup_inputs(seed: int = 0) -> dict:
    key_list = jax.random.split(jax.random.key(seed), 5)
    cost_volume = draw_cost_volume(jax.random.fold_in(key_list[4], 71), 0)
    left_image = gaussian(key_list[1], (H, W), 1.0, 6.0, ((0, 4), (1, 8)), jnp.float32)
    p_small = with_ends(jax.random.randint(key_list[2], (4,), 4, 17), jax.random.fold_in(key_list[2], 1), 4, 16).astype(jnp.int32)
    p_large = with_ends(jax.random.randint(key_list[3], (4,), 32, 129), jax.random.fold_in(key_list[3], 1), 32, 128).astype(jnp.int32)
    return {"cost_volume": cost_volume, "left_image": left_image, "p_small": p_small, "p_large": p_large}


FAR = 1.0e30
GRADIENT_GAIN = 4.0
OUT_SCALE = 1.0 / 256.0


def advance(previous, inputs, penalty_one):
    cost_line, large_line = inputs
    lowest = jnp.min(previous, axis=-1, keepdims=True)
    padded = jnp.pad(previous, ((0, 0), (1, 1)), constant_values=FAR)
    neighbour = jnp.minimum(padded[:, :-2], padded[:, 2:]) + penalty_one
    chosen = jnp.minimum(jnp.minimum(previous, neighbour), lowest + large_line[:, None])
    updated = cost_line.astype(jnp.float32) + chosen - lowest
    return updated, updated


def sweep(cost_lines, large_lines, penalty_one, start, backward):
    boundary, path_part = lax.scan(partial(advance, penalty_one=penalty_one), start, (cost_lines, large_lines), reverse=backward)
    return path_part, boundary


def adaptive(penalty_one, penalty_two, step_diff):
    return penalty_one + (penalty_two - penalty_one) / (1.0 + GRADIENT_GAIN * jnp.abs(step_diff))


def reference(cost_volume, left_image, p_small, p_large):
    padded = jnp.pad(left_image, 1)
    middle = padded[1:-1, 1:-1]
    small_pens = p_small.astype(jnp.float32)
    large_pens = p_large.astype(jnp.float32)
    penalty_right = adaptive(small_pens[0], large_pens[0], middle - padded[1:-1, :-2]).T
    penalty_left = adaptive(small_pens[1], large_pens[1], middle - padded[1:-1, 2:]).T
    penalty_down = adaptive(small_pens[2], large_pens[2], middle - padded[:-2, 1:-1])
    penalty_up = adaptive(small_pens[3], large_pens[3], middle - padded[2:, 1:-1])
    disparities = cost_volume.shape[2]
    crossed = jnp.transpose(cost_volume, (1, 0, 2))
    start_rows = jnp.zeros((crossed.shape[1], disparities), jnp.float32)
    start_cols = jnp.zeros((cost_volume.shape[1], disparities), jnp.float32)
    path_right, _ = sweep(crossed, penalty_right, small_pens[0], start_rows, False)
    path_left, _ = sweep(crossed, penalty_left, small_pens[1], start_rows, True)
    across = path_right + path_left
    path_down, _ = sweep(cost_volume, penalty_down, small_pens[2], start_cols, False)
    path_up, _ = sweep(cost_volume, penalty_up, small_pens[3], start_cols, True)
    down_total = path_down + path_up
    return (down_total + jnp.transpose(across, (1, 0, 2))) * OUT_SCALE
```

```python
import functools

import jax
import jax.numpy as jnp
from jax import lax
from jax.experimental import pallas as pl
from jax.experimental.pallas import tpu as pltpu
from jax.sharding import PartitionSpec as P

FAR = 1e30
GRADIENT_GAIN = 4.0
OUT_SCALE = 1.0 / 256.0
LANES = 128
SUBLANES = 8
BATCH = 4
UNROLL = 2
CORES = 2
VMEM_BYTES = 40 << 20
MESH = pl.DeviceIdType.MESH


def tree_min(parts):
    parts = list(parts)
    while len(parts) > 1:
        pairs = [jnp.minimum(a, b) for a, b in zip(parts[::2], parts[1::2])]
        parts = pairs + ([parts[-1]] if len(parts) % 2 else [])
    return parts[0]


def all_sublanes_min(x):
    for by in (4, 2, 1):
        x = jnp.minimum(x, pltpu.roll(x, by, 0))
    return x


def kernel(
    rows,
    cols,
    cost_hbm,
    image_hbm,
    small_hbm,
    large_hbm,
    out_ref,
    small_ref,
    large_ref,
    own_image,
    mate_image,
    own_raw,
    mate_raw,
    far_raw,
    ordered,
    ordered_other,
    order,
    totals,
    across_costs,
    down_costs,
    paths,
    lowests,
    large_lines,
    image_lines,
    outbox,
    inbox,
    edge_out,
    edge_in,
    send_sems,
    recv_sems,
    local_sems,
):
    disparities = cost_hbm.shape[1]
    nv = disparities // SUBLANES
    halves = disparities // LANES
    nx, ny = lax.axis_size("gx"), lax.axis_size("gy")
    ix, iy = lax.axis_index("gx"), lax.axis_index("gy")
    nz = nx // CORES
    iz, core = ix // CORES, ix % CORES
    mate = {"gx": iz * CORES + 1 - core}
    own_base = core * cols
    costs = (across_costs, down_costs)
    lengths = (cols, cols, rows, rows)
    lines = (rows, rows, cols, cols)
    backward = (False, True, False, True)

    place = (iz, nz - 1 - iz, iy, ny - 1 - iy)
    places = (nz, nz, ny, ny)
    hands_on = (core == 1, core == 0, True, True)
    is_last = [place[k] == places[k] - 1 for k in range(4)]
    skips = (False, False, places[2] > 1, places[3] > 1)

    def next_across(k, to_core):
        step = -1 if backward[k] else 1
        return {"gx": (iz + step) * CORES + to_core}

    def next_down(k, by):
        return {"gy": iy - by if backward[k] else iy + by}

    def prev_across(k):
        return {"gx": (iz + 1) * CORES if backward[k] else (iz - 1) * CORES + 1}

    def both(*flags):
        result = True
        for flag in flags:
            result = flag if result is True else jnp.logical_and(result, flag)
        return result

    def remote(source, target, send, recv, device):
        return pltpu.make_async_remote_copy(
            src_ref=source,
            dst_ref=target,
            send_sem=send_sems.at[send],
            recv_sem=recv_sems.at[recv],
            device_id=device,
            device_id_type=MESH,
        )

    mate_copies = [
        (None, remote(own_image, mate_image, 0, 0, mate)),
        (None, remote(own_raw, mate_raw, 1, 1, mate)),
    ]
    edge_copies, path_copies = [], []
    edge_recv, path_recv, far_recv = [], [], []
    far_raw_copies, far_large_copies = {}, {}
    for k in range(4):
        if k < 2:
            has_next = jnp.logical_and(place[k] < places[k] - 1, hands_on[k])
            e = [
                (has_next, remote(edge_out.at[k], edge_in.at[k], 2 + 2 * k + to, 2 + k, next_across(k, to)))
                for to in range(CORES)
            ]
            p = [
                (has_next, remote(outbox.at[k], inbox.at[k], 10 + 2 * k + to, 6 + k, next_across(k, to)))
                for to in range(CORES)
            ]
        else:
            has_next = place[k] < places[k] - 1
            e = [(has_next, remote(edge_out.at[k], edge_in.at[k], 2 + 2 * k, 2 + k, next_down(k, 1)))]
            p = [
                (
                    place[k] < places[k] - 2,
                    remote(outbox.at[k], inbox.at[k], 10 + 2 * k, 6 + k, next_down(k, 1)),
                ),
                (
                    place[k] == places[k] - 3,
                    remote(outbox.at[k], inbox.at[k], 11 + 2 * k, 6 + k, next_down(k, 2)),
                ),
            ]
            before_last = place[k] == places[k] - 2
            far_raw_copies[k] = (before_last, remote(own_raw, far_raw, 18 + k - 2, 10, next_down(k, 1)))
            far_large_copies[k] = (
                before_last,
                remote(
                    large_lines.at[k, pl.ds(rows, rows)],
                    large_lines.at[k, pl.ds(0, rows)],
                    20 + k - 2,
                    11,
                    next_down(k, 1),
                ),
            )
        edge_copies.append(e)
        path_copies.append(p)

    def start(copies):
        for flag, copy in copies:
            if flag is None:
                copy.start()
            else:
                pl.when(flag)(copy.start)

    def drain(copies):
        for flag, copy in copies:
            if flag is None:
                copy.wait_send()
            else:
                pl.when(flag)(copy.wait_send)

    locals_ = [
        pltpu.make_async_copy(source, target, local_sems.at[at])
        for at, (source, target) in enumerate(
            (
                (image_hbm, own_image),
                (small_hbm, small_ref),
                (large_hbm, large_ref),
                (cost_hbm, own_raw),
            )
        )
    ]
    for copy in locals_:
        copy.start()

    barrier = pltpu.get_barrier_semaphore()

    def greet(device):
        pl.semaphore_signal(barrier, inc=1, device_id=device, device_id_type=MESH)

    greet(mate)
    awaited = jnp.int32(1)
    for k in range(2):
        pl.when(place[k] > 0)(functools.partial(greet, prev_across(k)))
        sends = jnp.logical_and(place[k] < places[k] - 1, hands_on[k])
        awaited += jnp.where(sends, CORES, 0)
    for k in range(2, 4):
        pl.when(place[k] > 0)(functools.partial(greet, next_down(k, -1)))
        pl.when(jnp.logical_and(is_last[k], place[k] > 1))(
            functools.partial(greet, next_down(k, -2))
        )
        awaited += jnp.where(place[k] < places[k] - 1, 1, 0)
        awaited += jnp.where(place[k] == places[k] - 3, 1, 0)

    shape = (disparities, disparities)
    source = lax.broadcasted_iota(jnp.int32, shape, 0)
    target = lax.broadcasted_iota(jnp.int32, shape, 1)
    wanted = target // SUBLANES + nv * (target % SUBLANES)
    order[...] = jnp.where(source == wanted, 1.0, 0.0).astype(jnp.bfloat16)

    for copy in locals_[:3]:
        copy.wait()
    image = own_image[...]
    image_lines[...] = jnp.zeros_like(image_lines)
    image_lines[1, 0:rows, :cols] = image
    image_lines[0, pl.ds(pl.multiple_of(own_base, SUBLANES), cols), :rows] = image.T
    edge_out[...] = jnp.zeros_like(edge_out)
    edge_out[0, 0:1, :rows] = image.T[cols - 1 : cols, :]
    edge_out[1, 0:1, :rows] = image.T[0:1, :]
    edge_out[2, 0:1, :cols] = image[rows - 1 : rows, :]
    edge_out[3, 0:1, :cols] = image[0:1, :]
    locals_[3].wait()

    def reorder(raw, into):
        block = raw[...].astype(jnp.float32).astype(jnp.bfloat16)
        block = jnp.dot(block, order[...], preferred_element_type=jnp.float32)
        for h in range(halves):
            into[h] = block[:, h * LANES : (h + 1) * LANES]

    def turn_in(origin, into, line, at, count):
        per = LANES // SUBLANES
        for h in range(halves):
            block = origin[h, at, :].T.reshape(per, SUBLANES, count)
            into[line, h * per : (h + 1) * per, :, :count] = block

    def turn_across(origin, base):
        def some(index, carry):
            for slot in range(BATCH):
                line = index * BATCH + slot
                turn_in(origin, across_costs, base + line, pl.ds(line, rows, stride=cols), rows)
            return carry

        lax.fori_loop(0, cols // BATCH, some, 0)

    def turn_down(origin, base):
        def some(index, carry):
            for slot in range(BATCH):
                line = index * BATCH + slot
                at = pl.ds(pl.multiple_of(line * cols, cols), cols)
                turn_in(origin, down_costs, base + line, at, cols)
            return carry

        lax.fori_loop(0, rows // BATCH, some, 0)

    pl.semaphore_wait(barrier, awaited)
    start(mate_copies)
    for k in range(4):
        start(edge_copies[k])
    for k in range(2, 4):
        start([far_raw_copies[k]])

    reorder(own_raw, ordered)
    turn_down(ordered, rows)
    turn_across(ordered, own_base)

    sub = lax.broadcasted_iota(jnp.int32, (SUBLANES, LANES), 0)
    lane = lax.broadcasted_iota(jnp.int32, (SUBLANES, LANES), 1)

    def turn_back(registers, count):
        per = LANES // SUBLANES
        return [
            jnp.concatenate(registers[h * per : (h + 1) * per], axis=0)[:, :count].T
            for h in range(halves)
        ]

    def task(k):
        axis = k // 2
        length, width = lengths[k], lines[k]
        group = LANES // width
        small = small_ref[k].astype(jnp.float32)
        large = large_ref[k].astype(jnp.float32)
        step_costs = costs[axis]
        first = place[k] == 0

        @pl.when(jnp.logical_not(first))
        def _():
            edge_copies[k][0][1].wait_recv()

        @pl.when(first)
        def _():
            edge_in[k] = jnp.zeros((SUBLANES, LANES), jnp.float32)

        edge = edge_in[k, 0:1, :]
        if axis == 0:
            own = image_lines[0, : 2 * length, :]
        else:
            own = image_lines[1, :length, :]
        if backward[k]:
            before = jnp.concatenate([own[1:], edge], axis=0)
        else:
            before = jnp.concatenate([edge, own[:-1]], axis=0)
        found = small + (large - small) / (1.0 + GRADIENT_GAIN * jnp.abs(own - before))
        if axis == 0:
            large_lines[k, : 2 * length] = found
        else:
            large_lines[k, length : 2 * length] = found
            start([far_large_copies[k]])

            @pl.when(jnp.logical_and(is_last[k], jnp.logical_not(first)))
            def _():
                far_raw_copies[k][1].wait_recv()
                reorder(far_raw, ordered_other)
                turn_down(ordered_other, 0)
                far_large_copies[k][1].wait_recv()

        if axis == 0:
            receives = jnp.logical_not(first)
        else:
            receives = jnp.logical_or(
                jnp.logical_and(place[k] > 0, jnp.logical_not(is_last[k])),
                jnp.logical_and(is_last[k], place[k] > 1),
            )

        @pl.when(receives)
        def _():
            path_copies[k][0][1].wait_recv()

        @pl.when(jnp.logical_not(receives))
        def _():
            inbox[k] = jnp.zeros(inbox.shape[1:], jnp.float32)

        state = []
        for v in range(nv):
            packed = inbox[k, v // group]
            shift = (v % group) * width
            state.append(pltpu.roll(packed, LANES - shift, 1) if shift else packed)

        def step(line, state):
            capped = large_lines[k, pl.ds(line, SUBLANES, stride=0), :]
            under = jnp.where(sub == 0, FAR, pltpu.roll(state[-1], 1, 0))
            over = jnp.where(sub == SUBLANES - 1, FAR, pltpu.roll(state[0], SUBLANES - 1, 0))
            beside = []
            for v in range(nv):
                low = state[v - 1] if v else under
                high = state[v + 1] if v < nv - 1 else over
                beside.append(jnp.minimum(low, high))
            if nv % 4 == 0:
                lowest = tree_min([beside[v] for v in range(nv) if v % 4 in (1, 2)])
            else:
                lowest = tree_min(state)
            lowest = all_sublanes_min(lowest)
            capped = capped + lowest
            fresh = []
            for v in range(nv):
                near = jnp.minimum(state[v], beside[v] + small)
                fresh.append(step_costs[line, v] + jnp.minimum(near, capped))
            return tuple(fresh), lowest

        def early(index, state):
            for part in range(UNROLL):
                at = index * UNROLL + part
                if axis == 0:
                    line = 2 * length - 1 - at if backward[k] else at
                else:
                    line = length - 1 - at if backward[k] else at
                state, _ = step(line, state)
            return state

        def late(index, state):
            for part in range(UNROLL):
                at = index * UNROLL + part
                at = length - 1 - at if backward[k] else at
                state, lowest = step((own_base if axis == 0 else length) + at, state)
                for v in range(nv):
                    paths[k, at, v] = state[v]
                lowests[k, at] = lowest
            return state

        if axis == 0:
            ahead = jnp.where(hands_on[k], length // UNROLL, 0)
        else:
            ahead = jnp.where(jnp.logical_and(is_last[k], place[k] > 0), length // UNROLL, 0)
        state = lax.fori_loop(0, ahead, early, tuple(state))
        state = lax.fori_loop(0, length // UNROLL, late, tuple(state))

        if axis == 0:
            sends = path_copies[k][0][0]
        else:
            sends = jnp.logical_or(path_copies[k][0][0], path_copies[k][1][0])

        @pl.when(sends)
        def _():
            above = lowests[k, 0 if backward[k] else length - 1]
            sent = [part - above for part in state]
            for slot in range(nv // group):
                packed = sent[slot * group]
                for g in range(1, group):
                    moved = pltpu.roll(sent[slot * group + g], g * width, 1)
                    packed = jnp.where(lane >= g * width, moved, packed)
                outbox[k, slot] = packed

        start(path_copies[k])

    def both_ways(k, line, count):
        above = lowests[k, line] + lowests[k + 1, line]
        return turn_back(
            [paths[k, line, v] + paths[k + 1, line, v] - above for v in range(nv)], count
        )

    def down_total():
        def some(index, carry):
            for slot in range(BATCH):
                line = index * BATCH + slot
                at = pl.ds(pl.multiple_of(line * cols, cols), cols)
                for h, part in enumerate(both_ways(2, line, cols)):
                    totals[1, h, at, :] = part
            return carry

        lax.fori_loop(0, rows // BATCH, some, 0)

    def across_total():
        def some(index, carry):
            for slot in range(BATCH):
                line = index * BATCH + slot
                at = pl.ds(line, rows, stride=cols)
                for h, part in enumerate(both_ways(0, line, rows)):
                    totals[0, h, at, :] = part
            return carry

        lax.fori_loop(0, cols // BATCH, some, 0)

    turns = max(nz, ny)
    down_done = jnp.maximum(place[2], place[3])

    def one_turn(turn, carry):
        pl.when(turn == place[2])(lambda: task(2))
        pl.when(turn == place[3])(lambda: task(3))

        @pl.when(turn == 0)
        def _():
            for _, copy in mate_copies:
                copy.wait_recv()
            at = pl.ds(pl.multiple_of(cols - own_base, SUBLANES), cols)
            image_lines[0, at, :rows] = mate_image[...].T
            reorder(mate_raw, ordered_other)
            turn_across(ordered_other, cols - own_base)

        at_end = jnp.logical_and(turn == down_done, turn == turns - 1)
        pl.when(at_end)(down_total)
        pl.when(turn == place[0])(lambda: task(0))
        pl.when(turn == place[1])(lambda: task(1))
        before_end = jnp.logical_and(turn == down_done, turn < turns - 1)
        pl.when(before_end)(down_total)
        return carry

    lax.fori_loop(0, turns, one_turn, 0)
    across_total()
    rest = jnp.concatenate([totals[0, h] + totals[1, h] for h in range(halves)], axis=1)
    rest = rest * OUT_SCALE
    result = None
    for part in range(3):
        piece = rest.astype(jnp.bfloat16)
        moved = lax.dot_general(
            piece, order[...], (((1,), (1,)), ((), ())), preferred_element_type=jnp.float32
        )
        result = moved if part == 0 else result + moved
        if part < 2:
            rest = rest - piece.astype(jnp.float32)
    out_ref[...] = result

    drain(mate_copies)
    for k in range(4):
        drain(edge_copies[k])
        drain(path_copies[k])
    for k in range(2, 4):
        drain([far_raw_copies[k], far_large_copies[k]])


def on_device(cost_volume, left_image, p_small, p_large):
    rows, cols, disparities = cost_volume.shape
    nv = disparities // SUBLANES
    longest = max(rows, cols)
    packed = nv * longest // LANES
    halves = disparities // LANES
    block = (rows * cols, disparities)
    hbm = pl.BlockSpec(memory_space=pltpu.HBM)
    vmem = pl.BlockSpec(memory_space=pltpu.VMEM)
    total = pl.pallas_call(
        functools.partial(kernel, rows, cols),
        out_shape=jax.ShapeDtypeStruct((rows * cols, disparities), jnp.float32),
        in_specs=[hbm] * 4,
        out_specs=vmem,
        scratch_shapes=[
            pltpu.SMEM((4,), jnp.int32),
            pltpu.SMEM((4,), jnp.int32),
            pltpu.VMEM((rows, cols), jnp.float32),
            pltpu.VMEM((rows, cols), jnp.float32),
            pltpu.VMEM(block, jnp.int32),
            pltpu.VMEM(block, jnp.int32),
            pltpu.VMEM(block, jnp.int32),
            pltpu.VMEM((halves, rows * cols, LANES), jnp.float32),
            pltpu.VMEM((halves, rows * cols, LANES), jnp.float32),
            pltpu.VMEM((disparities, disparities), jnp.bfloat16),
            pltpu.VMEM((2, halves, rows * cols, LANES), jnp.float32),
            pltpu.VMEM((2 * cols, nv, SUBLANES, LANES), jnp.float32),
            pltpu.VMEM((2 * rows, nv, SUBLANES, LANES), jnp.float32),
            pltpu.VMEM((4, longest, nv, SUBLANES, LANES), jnp.float32),
            pltpu.VMEM((4, longest, SUBLANES, LANES), jnp.float32),
            pltpu.VMEM((4, 2 * longest, LANES), jnp.float32),
            pltpu.VMEM((2, 2 * longest, LANES), jnp.float32),
            pltpu.VMEM((4, packed, SUBLANES, LANES), jnp.float32),
            pltpu.VMEM((4, packed, SUBLANES, LANES), jnp.float32),
            pltpu.VMEM((4, SUBLANES, LANES), jnp.float32),
            pltpu.VMEM((4, SUBLANES, LANES), jnp.float32),
            pltpu.SemaphoreType.DMA((22,)),
            pltpu.SemaphoreType.DMA((12,)),
            pltpu.SemaphoreType.DMA((4,)),
        ],
        compiler_params=pltpu.CompilerParams(
            collective_id=0, has_side_effects=True, vmem_limit_bytes=VMEM_BYTES
        ),
    )(
        *(
            pltpu.with_memory_space_constraint(array, pltpu.HBM)
            for array in (
                cost_volume.reshape(rows * cols, disparities),
                left_image,
                p_small,
                p_large,
            )
        )
    )
    return total.reshape(rows, cols, disparities)


def solution(mesh):
    in_specs = (P("gy", "gx", None), P("gy", "gx"), P(), P())
    out_specs = P("gy", "gx", None)
    return jax.shard_map(
        on_device, mesh=mesh, in_specs=in_specs, out_specs=out_specs, check_vma=False
    )
```

```python
import functools

import jax
import jax.numpy as jnp
from jax import lax
from jax.experimental import pallas as pl
from jax.experimental.pallas import tpu as pltpu
from jax.sharding import PartitionSpec as P

FAR = 1e30
GRADIENT_GAIN = 4.0
OUT_SCALE = 1.0 / 256.0
LANES = 128
SUBLANES = 8
BATCH = 4
UNROLL = 2
CORES = 2
VMEM_BYTES = 40 << 20
MESH = pl.DeviceIdType.MESH


def tree_min(parts):
    parts = list(parts)
    while len(parts) > 1:
        pairs = [jnp.minimum(a, b) for a, b in zip(parts[::2], parts[1::2])]
        parts = pairs + ([parts[-1]] if len(parts) % 2 else [])
    return parts[0]


def all_sublanes_min(x):
    for by in (4, 2, 1):
        x = jnp.minimum(x, pltpu.roll(x, by, 0))
    return x


def kernel(
    rows,
    cols,
    cost_hbm,
    image_hbm,
    small_hbm,
    large_hbm,
    out_ref,
    small_ref,
    large_ref,
    own_image,
    mate_image,
    own_raw,
    mate_raw,
    far_raw,
    order,
    totals,
    across_costs,
    down_costs,
    paths,
    lowests,
    large_lines,
    image_lines,
    outbox,
    inbox,
    edge_out,
    edge_in,
    send_sems,
    recv_sems,
    local_sems,
):
    disparities = cost_hbm.shape[1]
    nv = disparities // SUBLANES
    halves = disparities // LANES
    nx, ny = lax.axis_size("gx"), lax.axis_size("gy")
    ix, iy = lax.axis_index("gx"), lax.axis_index("gy")
    nz = nx // CORES
    iz, core = ix // CORES, ix % CORES
    mate = {"gx": iz * CORES + 1 - core}
    own_base = core * cols
    costs = (across_costs, down_costs)
    lengths = (cols, cols, rows, rows)
    lines = (rows, rows, cols, cols)
    backward = (False, True, False, True)

    place = (iz, nz - 1 - iz, iy, ny - 1 - iy)
    places = (nz, nz, ny, ny)
    hands_on = (core == 1, core == 0, True, True)
    is_last = [place[k] == places[k] - 1 for k in range(4)]
    skips = (False, False, places[2] > 1, places[3] > 1)

    def next_across(k, to_core):
        step = -1 if backward[k] else 1
        return {"gx": (iz + step) * CORES + to_core}

    def next_down(k, by):
        return {"gy": iy - by if backward[k] else iy + by}

    def prev_across(k):
        return {"gx": (iz + 1) * CORES if backward[k] else (iz - 1) * CORES + 1}

    def both(*flags):
        result = True
        for flag in flags:
            result = flag if result is True else jnp.logical_and(result, flag)
        return result

    def remote(source, target, send, recv, device):
        return pltpu.make_async_remote_copy(
            src_ref=source,
            dst_ref=target,
            send_sem=send_sems.at[send],
            recv_sem=recv_sems.at[recv],
            device_id=device,
            device_id_type=MESH,
        )

    mate_copies = [
        (None, remote(own_image, mate_image, 0, 0, mate)),
        (None, remote(own_raw, mate_raw, 1, 1, mate)),
    ]
    edge_copies, path_copies = [], []
    edge_recv, path_recv, far_recv = [], [], []
    far_raw_copies, far_large_copies = {}, {}
    for k in range(4):
        if k < 2:
            has_next = jnp.logical_and(place[k] < places[k] - 1, hands_on[k])
            e = [
                (has_next, remote(edge_out.at[k], edge_in.at[k], 2 + 2 * k + to, 2 + k, next_across(k, to)))
                for to in range(CORES)
            ]
            p = [
                (has_next, remote(outbox.at[k], inbox.at[k], 10 + 2 * k + to, 6 + k, next_across(k, to)))
                for to in range(CORES)
            ]
        else:
            has_next = place[k] < places[k] - 1
            e = [(has_next, remote(edge_out.at[k], edge_in.at[k], 2 + 2 * k, 2 + k, next_down(k, 1)))]
            p = [
                (
                    place[k] < places[k] - 2,
                    remote(outbox.at[k], inbox.at[k], 10 + 2 * k, 6 + k, next_down(k, 1)),
                ),
                (
                    place[k] == places[k] - 3,
                    remote(outbox.at[k], inbox.at[k], 11 + 2 * k, 6 + k, next_down(k, 2)),
                ),
            ]
            before_last = place[k] == places[k] - 2
            far_raw_copies[k] = (before_last, remote(own_raw, far_raw, 18 + k - 2, 10, next_down(k, 1)))
            far_large_copies[k] = (
                before_last,
                remote(
                    large_lines.at[k, pl.ds(rows, rows)],
                    large_lines.at[k, pl.ds(0, rows)],
                    20 + k - 2,
                    11,
                    next_down(k, 1),
                ),
            )
        edge_copies.append(e)
        path_copies.append(p)

    def start(copies):
        for flag, copy in copies:
            if flag is None:
                copy.start()
            else:
                pl.when(flag)(copy.start)

    def drain(copies):
        for flag, copy in copies:
            if flag is None:
                copy.wait_send()
            else:
                pl.when(flag)(copy.wait_send)

    locals_ = [
        pltpu.make_async_copy(source, target, local_sems.at[at])
        for at, (source, target) in enumerate(
            (
                (image_hbm, own_image),
                (small_hbm, small_ref),
                (large_hbm, large_ref),
                *(
                    (cost_hbm.at[:, pl.ds(h * LANES, LANES)], own_raw.at[h])
                    for h in range(halves)
                ),
            )
        )
    ]
    for copy in locals_:
        copy.start()

    barrier = pltpu.get_barrier_semaphore()

    def greet(device):
        pl.semaphore_signal(barrier, inc=1, device_id=device, device_id_type=MESH)

    greet(mate)
    awaited = jnp.int32(1)
    for k in range(2):
        pl.when(place[k] > 0)(functools.partial(greet, prev_across(k)))
        sends = jnp.logical_and(place[k] < places[k] - 1, hands_on[k])
        awaited += jnp.where(sends, CORES, 0)
    for k in range(2, 4):
        pl.when(place[k] > 0)(functools.partial(greet, next_down(k, -1)))
        pl.when(jnp.logical_and(is_last[k], place[k] > 1))(
            functools.partial(greet, next_down(k, -2))
        )
        awaited += jnp.where(place[k] < places[k] - 1, 1, 0)
        awaited += jnp.where(place[k] == places[k] - 3, 1, 0)

    shape = (disparities, disparities)
    source = lax.broadcasted_iota(jnp.int32, shape, 1)
    target = lax.broadcasted_iota(jnp.int32, shape, 0)
    wanted = target // SUBLANES + nv * (target % SUBLANES)
    order[...] = jnp.where(source == wanted, 1.0, 0.0).astype(jnp.bfloat16)

    for copy in locals_[:3]:
        copy.wait()
    image = own_image[...]
    image_lines[...] = jnp.zeros_like(image_lines)
    image_lines[1, 0:rows, :cols] = image
    image_lines[0, pl.ds(pl.multiple_of(own_base, SUBLANES), cols), :rows] = image.T
    edge_out[...] = jnp.zeros_like(edge_out)
    edge_out[0, 0:1, :rows] = image.T[cols - 1 : cols, :]
    edge_out[1, 0:1, :rows] = image.T[0:1, :]
    edge_out[2, 0:1, :cols] = image[rows - 1 : rows, :]
    edge_out[3, 0:1, :cols] = image[0:1, :]
    for copy in locals_[3:]:
        copy.wait()

    def turn_in(origin, into, line, at, count):
        block = jnp.concatenate([origin[h, at, :] for h in range(halves)], axis=1)
        block = block.astype(jnp.float32).astype(jnp.bfloat16)
        block = lax.dot_general(
            order[...], block, (((1,), (1,)), ((), ())), preferred_element_type=jnp.float32
        )
        into[line, :, :, :count] = block.reshape(nv, SUBLANES, count)

    def turn_across(origin, base):
        def some(index, carry):
            for slot in range(BATCH):
                line = index * BATCH + slot
                turn_in(origin, across_costs, base + line, pl.ds(line, rows, stride=cols), rows)
            return carry

        lax.fori_loop(0, cols // BATCH, some, 0)

    def turn_down(origin, base):
        def some(index, carry):
            for slot in range(BATCH):
                line = index * BATCH + slot
                at = pl.ds(pl.multiple_of(line * cols, cols), cols)
                turn_in(origin, down_costs, base + line, at, cols)
            return carry

        lax.fori_loop(0, rows // BATCH, some, 0)

    def take_mate():
        for _, copy in mate_copies:
            copy.wait_recv()
        at = pl.ds(pl.multiple_of(cols - own_base, SUBLANES), cols)
        image_lines[0, at, :rows] = mate_image[...].T
        turn_across(mate_raw, cols - own_base)

    @pl.when(iz < nz - 1)
    def _():
        turn_down(own_raw, rows)
        turn_across(own_raw, own_base)

    pl.semaphore_wait(barrier, awaited)
    start(mate_copies)
    for k in range(4):
        start(edge_copies[k])
    for k in range(2, 4):
        start([far_raw_copies[k]])

    @pl.when(iz == nz - 1)
    def _():
        turn_across(own_raw, own_base)
        take_mate()

    sub = lax.broadcasted_iota(jnp.int32, (SUBLANES, LANES), 0)
    lane = lax.broadcasted_iota(jnp.int32, (SUBLANES, LANES), 1)

    def turn_back(registers, count):
        per = LANES // SUBLANES
        return [
            jnp.concatenate(registers[h * per : (h + 1) * per], axis=0)[:, :count].T
            for h in range(halves)
        ]

    def task(k):
        axis = k // 2
        length, width = lengths[k], lines[k]
        group = LANES // width
        small = small_ref[k].astype(jnp.float32)
        large = large_ref[k].astype(jnp.float32)
        step_costs = costs[axis]
        first = place[k] == 0

        @pl.when(jnp.logical_not(first))
        def _():
            edge_copies[k][0][1].wait_recv()

        @pl.when(first)
        def _():
            edge_in[k] = jnp.zeros((SUBLANES, LANES), jnp.float32)

        edge = edge_in[k, 0:1, :]
        if axis == 0:
            own = image_lines[0, : 2 * length, :]
        else:
            own = image_lines[1, :length, :]
        if backward[k]:
            before = jnp.concatenate([own[1:], edge], axis=0)
        else:
            before = jnp.concatenate([edge, own[:-1]], axis=0)
        found = small + (large - small) / (1.0 + GRADIENT_GAIN * jnp.abs(own - before))
        if axis == 0:
            large_lines[k, : 2 * length] = found
        else:
            large_lines[k, length : 2 * length] = found
            start([far_large_copies[k]])

            @pl.when(jnp.logical_and(is_last[k], jnp.logical_not(first)))
            def _():
                far_raw_copies[k][1].wait_recv()
                turn_down(far_raw, 0)
                far_large_copies[k][1].wait_recv()

        if axis == 0:
            receives = jnp.logical_not(first)
        else:
            receives = jnp.logical_or(
                jnp.logical_and(place[k] > 0, jnp.logical_not(is_last[k])),
                jnp.logical_and(is_last[k], place[k] > 1),
            )

        @pl.when(receives)
        def _():
            path_copies[k][0][1].wait_recv()

        @pl.when(jnp.logical_not(receives))
        def _():
            inbox[k] = jnp.zeros(inbox.shape[1:], jnp.float32)

        state = []
        for v in range(nv):
            packed = inbox[k, v // group]
            shift = (v % group) * width
            state.append(pltpu.roll(packed, LANES - shift, 1) if shift else packed)

        def step(line, state):
            capped = large_lines[k, pl.ds(line, SUBLANES, stride=0), :]
            under = jnp.where(sub == 0, FAR, pltpu.roll(state[-1], 1, 0))
            over = jnp.where(sub == SUBLANES - 1, FAR, pltpu.roll(state[0], SUBLANES - 1, 0))
            beside = []
            for v in range(nv):
                low = state[v - 1] if v else under
                high = state[v + 1] if v < nv - 1 else over
                beside.append(jnp.minimum(low, high))
            if nv % 4 == 0:
                lowest = tree_min([beside[v] for v in range(nv) if v % 4 in (1, 2)])
            else:
                lowest = tree_min(state)
            lowest = all_sublanes_min(lowest)
            capped = capped + lowest
            fresh = []
            for v in range(nv):
                near = jnp.minimum(state[v], beside[v] + small)
                fresh.append(step_costs[line, v] + jnp.minimum(near, capped))
            return tuple(fresh), lowest

        def early(index, state):
            for part in range(UNROLL):
                at = index * UNROLL + part
                if axis == 0:
                    line = 2 * length - 1 - at if backward[k] else at
                else:
                    line = length - 1 - at if backward[k] else at
                state, _ = step(line, state)
            return state

        def late(index, state):
            for part in range(UNROLL):
                at = index * UNROLL + part
                at = length - 1 - at if backward[k] else at
                state, lowest = step((own_base if axis == 0 else length) + at, state)
                for v in range(nv):
                    paths[k, at, v] = state[v]
                lowests[k, at] = lowest
            return state

        if axis == 0:
            ahead = jnp.where(hands_on[k], length // UNROLL, 0)
        else:
            ahead = jnp.where(jnp.logical_and(is_last[k], place[k] > 0), length // UNROLL, 0)
        state = lax.fori_loop(0, ahead, early, tuple(state))
        state = lax.fori_loop(0, length // UNROLL, late, tuple(state))

        if axis == 0:
            sends = path_copies[k][0][0]
        else:
            sends = jnp.logical_or(path_copies[k][0][0], path_copies[k][1][0])

        @pl.when(sends)
        def _():
            above = lowests[k, 0 if backward[k] else length - 1]
            sent = [part - above for part in state]
            for slot in range(nv // group):
                packed = sent[slot * group]
                for g in range(1, group):
                    moved = pltpu.roll(sent[slot * group + g], g * width, 1)
                    packed = jnp.where(lane >= g * width, moved, packed)
                outbox[k, slot] = packed

        start(path_copies[k])

    def both_ways(k, line, count):
        above = lowests[k, line] + lowests[k + 1, line]
        return turn_back(
            [paths[k, line, v] + paths[k + 1, line, v] - above for v in range(nv)], count
        )

    def down_total():
        def some(index, carry):
            for slot in range(BATCH):
                line = index * BATCH + slot
                at = pl.ds(pl.multiple_of(line * cols, cols), cols)
                for h, part in enumerate(both_ways(2, line, cols)):
                    totals[1, h, at, :] = part
            return carry

        lax.fori_loop(0, rows // BATCH, some, 0)

    def across_total():
        def some(index, carry):
            for slot in range(BATCH):
                line = index * BATCH + slot
                at = pl.ds(line, rows, stride=cols)
                for h, part in enumerate(both_ways(0, line, rows)):
                    totals[0, h, at, :] = part
            return carry

        lax.fori_loop(0, cols // BATCH, some, 0)

    turns = max(nz, ny)
    down_done = jnp.maximum(place[2], place[3])
    turn_left = jnp.where(iz == 0, nz, place[1])

    def one_turn(turn, carry):
        pl.when(turn == turn_left)(lambda: task(1))
        pl.when(jnp.logical_and(turn == 0, iz == nz - 1))(lambda: turn_down(own_raw, rows))
        pl.when(turn == place[2])(lambda: task(2))
        pl.when(turn == place[3])(lambda: task(3))
        pl.when(jnp.logical_and(turn == 0, iz < nz - 1))(take_mate)
        pl.when(turn == down_done)(down_total)
        pl.when(turn == place[0])(lambda: task(0))
        return carry

    lax.fori_loop(0, turns + 1, one_turn, 0)
    across_total()
    rest = jnp.concatenate([totals[0, h] + totals[1, h] for h in range(halves)], axis=1)
    rest = rest * OUT_SCALE
    result = None
    for part in range(3):
        piece = rest.astype(jnp.bfloat16)
        moved = lax.dot_general(
            piece, order[...], (((1,), (0,)), ((), ())), preferred_element_type=jnp.float32
        )
        result = moved if part == 0 else result + moved
        if part < 2:
            rest = rest - piece.astype(jnp.float32)
    out_ref[...] = result

    drain(mate_copies)
    for k in range(4):
        drain(edge_copies[k])
        drain(path_copies[k])
    for k in range(2, 4):
        drain([far_raw_copies[k], far_large_copies[k]])


def on_device(cost_volume, left_image, p_small, p_large):
    rows, cols, disparities = cost_volume.shape
    nv = disparities // SUBLANES
    longest = max(rows, cols)
    packed = nv * longest // LANES
    halves = disparities // LANES
    block = (halves, rows * cols, LANES)
    hbm = pl.BlockSpec(memory_space=pltpu.HBM)
    vmem = pl.BlockSpec(memory_space=pltpu.VMEM)
    total = pl.pallas_call(
        functools.partial(kernel, rows, cols),
        out_shape=jax.ShapeDtypeStruct((rows * cols, disparities), jnp.float32),
        in_specs=[hbm] * 4,
        out_specs=vmem,
        scratch_shapes=[
            pltpu.SMEM((4,), jnp.int32),
            pltpu.SMEM((4,), jnp.int32),
            pltpu.VMEM((rows, cols), jnp.float32),
            pltpu.VMEM((rows, cols), jnp.float32),
            pltpu.VMEM(block, jnp.int32),
            pltpu.VMEM(block, jnp.int32),
            pltpu.VMEM(block, jnp.int32),
            pltpu.VMEM((disparities, disparities), jnp.bfloat16),
            pltpu.VMEM((2, halves, rows * cols, LANES), jnp.float32),
            pltpu.VMEM((2 * cols, nv, SUBLANES, LANES), jnp.float32),
            pltpu.VMEM((2 * rows, nv, SUBLANES, LANES), jnp.float32),
            pltpu.VMEM((4, longest, nv, SUBLANES, LANES), jnp.float32),
            pltpu.VMEM((4, longest, SUBLANES, LANES), jnp.float32),
            pltpu.VMEM((4, 2 * longest, LANES), jnp.float32),
            pltpu.VMEM((2, 2 * longest, LANES), jnp.float32),
            pltpu.VMEM((4, packed, SUBLANES, LANES), jnp.float32),
            pltpu.VMEM((4, packed, SUBLANES, LANES), jnp.float32),
            pltpu.VMEM((4, SUBLANES, LANES), jnp.float32),
            pltpu.VMEM((4, SUBLANES, LANES), jnp.float32),
            pltpu.SemaphoreType.DMA((22,)),
            pltpu.SemaphoreType.DMA((12,)),
            pltpu.SemaphoreType.DMA((3 + halves,)),
        ],
        compiler_params=pltpu.CompilerParams(
            collective_id=0, has_side_effects=True, vmem_limit_bytes=VMEM_BYTES
        ),
    )(
        *(
            pltpu.with_memory_space_constraint(array, pltpu.HBM)
            for array in (
                cost_volume.reshape(rows * cols, disparities),
                left_image,
                p_small,
                p_large,
            )
        )
    )
    return total.reshape(rows, cols, disparities)


def solution(mesh):
    in_specs = (P("gy", "gx", None), P("gy", "gx"), P(), P())
    out_specs = P("gy", "gx", None)
    return jax.shard_map(
        on_device, mesh=mesh, in_specs=in_specs, out_specs=out_specs, check_vma=False
    )
```

```python
import functools

import jax
import jax.numpy as jnp
from jax import lax
from jax.experimental import pallas as pl
from jax.experimental.pallas import tpu as pltpu
from jax.sharding import PartitionSpec as P

FAR = 1e30
GRADIENT_GAIN = 4.0
OUT_SCALE = 1.0 / 256.0
LANES = 128
SUBLANES = 8
UNROLL = 2
CORES = 2
SENDS = 30
VMEM_BYTES = 40 << 20
SKIPS = (False, True, True, True)
MESH = pl.DeviceIdType.MESH


def tree_min(parts):
    parts = list(parts)
    while len(parts) > 1:
        pairs = [jnp.minimum(a, b) for a, b in zip(parts[::2], parts[1::2])]
        parts = pairs + ([parts[-1]] if len(parts) % 2 else [])
    return parts[0]


def all_sublanes_min(x):
    for by in (4, 2, 1):
        x = jnp.minimum(x, pltpu.roll(x, by, 0))
    return x


def kernel(
    rows,
    cols,
    cost_hbm,
    image_hbm,
    small_hbm,
    large_hbm,
    out_ref,
    small_ref,
    large_ref,
    own_image,
    mate_image,
    own_raw,
    mate_raw,
    far_raw,
    far_across,
    order,
    totals,
    across_costs,
    down_costs,
    paths,
    lowests,
    large_lines,
    image_lines,
    outbox,
    inbox,
    edge_out,
    edge_in,
    send_sems,
    recv_sems,
    local_sems,
):
    disparities = cost_hbm.shape[1]
    nv = disparities // SUBLANES
    halves = disparities // LANES
    nx, ny = lax.axis_size("gx"), lax.axis_size("gy")
    ix, iy = lax.axis_index("gx"), lax.axis_index("gy")
    nz = nx // CORES
    iz, core = ix // CORES, ix % CORES
    mate = {"gx": iz * CORES + 1 - core}
    own_base = core * cols
    spans = (CORES * cols, rows)
    costs = (across_costs, down_costs)
    lengths = (cols, cols, rows, rows)
    lines = (rows, rows, cols, cols)
    backward = (False, True, False, True)

    place = (iz, nz - 1 - iz, iy, ny - 1 - iy)
    places = (nz, nz, ny, ny)
    hands_on = (core == 1, core == 0, True, True)
    is_last = [place[k] == places[k] - 1 for k in range(4)]

    def next_across(k, by, to_core):
        step = -by if backward[k] else by
        return {"gx": (iz + step) * CORES + to_core}

    def next_down(k, by):
        return {"gy": iy - by if backward[k] else iy + by}

    def prev_across(k, by):
        return next_across(k, -by, 0 if backward[k] else 1)

    def both(*flags):
        result = True
        for flag in flags:
            result = flag if result is True else jnp.logical_and(result, flag)
        return result

    sends = iter(range(SENDS))

    def remote(source, target, recv, device):
        return pltpu.make_async_remote_copy(
            src_ref=source,
            dst_ref=target,
            send_sem=send_sems.at[next(sends)],
            recv_sem=recv_sems.at[recv],
            device_id=device,
            device_id_type=MESH,
        )

    mate_copies = [
        (None, remote(own_image, mate_image, 0, mate)),
        (None, remote(own_raw, mate_raw, 1, mate)),
    ]
    edge_copies, path_copies, far_raw_copies, far_large_copies = [], [], [], []
    forward_copies = {}
    for k in range(4):
        sent = hands_on[k]
        after = places[k] - 1 - place[k]
        near_end = 2 if SKIPS[k] else 1
        if k < 2:
            to = lambda by, k=k: [next_across(k, by, c) for c in range(CORES)]
            same_core = next_across(k, 1, core)
        else:
            to = lambda by, k=k: [next_down(k, by)]
            same_core = next_down(k, 1)
        edge_copies.append(
            [
                (both(sent, after >= 1), remote(edge_out.at[k], edge_in.at[k], 2 + k, device))
                for device in to(1)
            ]
        )
        path_copies.append(
            [
                (both(sent, after >= near_end), remote(outbox.at[k], inbox.at[k], 6 + k, device))
                for device in to(1)
            ]
        )
        if SKIPS[k]:
            path_copies[k] += [
                (both(sent, after == 2), remote(outbox.at[k], inbox.at[k], 6 + k, device))
                for device in to(2)
            ]
            span = spans[k // 2]
            target = far_across.at[core] if k < 2 else far_raw
            far_raw_copies.append([(after == 1, remote(own_raw, target, 10 + k, same_core))])
            far_large_copies.append(
                [
                    (
                        after == 1,
                        remote(
                            large_lines.at[k, pl.ds(span, span)],
                            large_lines.at[k, pl.ds(0, span)],
                            14 + k,
                            same_core,
                        ),
                    )
                ]
            )
            if k < 2:
                here = far_across.at[core]
                forward_copies[k] = [(None, remote(here, here, 18 + k, mate))]
        else:
            far_raw_copies.append([])
            far_large_copies.append([])

    def start(copies):
        for flag, copy in copies:
            if flag is None:
                copy.start()
            else:
                pl.when(flag)(copy.start)

    def drain(copies):
        for flag, copy in copies:
            if flag is None:
                copy.wait_send()
            else:
                pl.when(flag)(copy.wait_send)

    locals_ = [
        pltpu.make_async_copy(source, target, local_sems.at[at])
        for at, (source, target) in enumerate(
            (
                (image_hbm, own_image),
                (small_hbm, small_ref),
                (large_hbm, large_ref),
                *(
                    (cost_hbm.at[:, pl.ds(h * LANES, LANES)], own_raw.at[h])
                    for h in range(halves)
                ),
            )
        )
    ]
    for copy in locals_:
        copy.start()

    barrier = pltpu.get_barrier_semaphore()

    def greet(device):
        pl.semaphore_signal(barrier, inc=1, device_id=device, device_id_type=MESH)

    greet(mate)
    awaited = jnp.int32(1)
    for k in range(4):
        after = places[k] - 1 - place[k]
        ends = both(after == 0, place[k] > 0)
        skips = both(after == 0, place[k] > 1)
        if k < 2:
            pl.when(place[k] > 0)(functools.partial(greet, prev_across(k, 1)))
            awaited += jnp.where(both(hands_on[k], after >= 1), CORES, 0)
            if SKIPS[k]:
                far_only = jnp.logical_not(hands_on[k])
                pl.when(both(ends, far_only))(
                    functools.partial(greet, next_across(k, -1, core))
                )
                awaited += jnp.where(both(far_only, after == 1), 1, 0)
                pl.when(skips)(functools.partial(greet, prev_across(k, 2)))
                awaited += jnp.where(both(hands_on[k], after == 2), CORES, 0)
        else:
            pl.when(place[k] > 0)(functools.partial(greet, next_down(k, -1)))
            awaited += jnp.where(after >= 1, 1, 0)
            if SKIPS[k]:
                pl.when(skips)(functools.partial(greet, next_down(k, -2)))
                awaited += jnp.where(after == 2, 1, 0)

    shape = (disparities, disparities)
    source = lax.broadcasted_iota(jnp.int32, shape, 1)
    target = lax.broadcasted_iota(jnp.int32, shape, 0)
    wanted = target // SUBLANES + nv * (target % SUBLANES)
    order[...] = jnp.where(source == wanted, 1.0, 0.0).astype(jnp.bfloat16)

    for copy in locals_[:3]:
        copy.wait()
    image = own_image[...]
    image_lines[...] = jnp.zeros_like(image_lines)
    image_lines[1, 0:rows, :cols] = image
    image_lines[0, pl.ds(pl.multiple_of(own_base, SUBLANES), cols), :rows] = image.T
    edge_out[...] = jnp.zeros_like(edge_out)
    edge_out[0, 0:1, :rows] = image.T[cols - 1 : cols, :]
    edge_out[1, 0:1, :rows] = image.T[0:1, :]
    edge_out[2, 0:1, :cols] = image[rows - 1 : rows, :]
    edge_out[3, 0:1, :cols] = image[0:1, :]
    for copy in locals_[3:]:
        copy.wait()

    def turn(origin, into, base, axis):
        width = lines[2 * axis]
        group = LANES // width

        def some(index, carry):
            first = index * group
            block = []
            for h in range(halves):
                if axis == 0:
                    parts = [
                        origin[h, pl.ds(first + j, width, stride=cols), :] for j in range(group)
                    ]
                    block.append(jnp.concatenate(parts, axis=0))
                else:
                    at = pl.ds(index * LANES, LANES)
                    block.append(origin[h, at, :])
            block = jnp.concatenate(block, axis=1).astype(jnp.float32).astype(jnp.bfloat16)
            block = lax.dot_general(
                order[...], block, (((1,), (1,)), ((), ())), preferred_element_type=jnp.float32
            )
            for j in range(group):
                moved = pltpu.roll(block, LANES - j * width, 1) if j else block
                into[base + first + j] = moved.reshape(nv, SUBLANES, LANES)
            return carry

        for index in range(rows * cols // LANES):
            some(index, None)

    def turn_across(origin, base):
        turn(origin, across_costs, base, 0)

    def turn_down(origin, base):
        turn(origin, down_costs, base, 1)

    def take_mate():
        for _, copy in mate_copies:
            copy.wait_recv()
        at = pl.ds(pl.multiple_of(cols - own_base, SUBLANES), cols)
        image_lines[0, at, :rows] = mate_image[...].T
        turn_across(mate_raw, spans[0] + cols - own_base)

    pl.semaphore_wait(barrier, awaited)
    start(mate_copies)
    for k in range(4):
        start(edge_copies[k])
    for k in range(4):
        start(far_raw_copies[k])

    pl.when(iz < nz - 1)(lambda: turn_down(own_raw, rows))
    turn_across(own_raw, spans[0] + own_base)
    pl.when(iz == nz - 1)(take_mate)

    sub = lax.broadcasted_iota(jnp.int32, (SUBLANES, LANES), 0)
    lane = lax.broadcasted_iota(jnp.int32, (SUBLANES, LANES), 1)

    def task(k):
        axis = k // 2
        length, width = lengths[k], lines[k]
        group = LANES // width
        small = small_ref[k].astype(jnp.float32)
        large = large_ref[k].astype(jnp.float32)
        step_costs = costs[axis]
        first = place[k] == 0

        @pl.when(jnp.logical_not(first))
        def _():
            edge_copies[k][0][1].wait_recv()

        @pl.when(first)
        def _():
            edge_in[k] = jnp.zeros((SUBLANES, LANES), jnp.float32)

        edge = edge_in[k, 0:1, :]
        if axis == 0:
            own = image_lines[0, : CORES * length, :]
        else:
            own = image_lines[1, :length, :]
        if backward[k]:
            before = jnp.concatenate([own[1:], edge], axis=0)
        else:
            before = jnp.concatenate([edge, own[:-1]], axis=0)
        found = small + (large - small) / (1.0 + GRADIENT_GAIN * jnp.abs(own - before))
        span = spans[axis]
        large_lines[k, span : 2 * span] = found
        start(far_large_copies[k])
        ends = both(is_last[k], jnp.logical_not(first)) if SKIPS[k] else False
        receives = jnp.logical_not(first)
        if SKIPS[k]:
            if axis == 1:

                @pl.when(ends)
                def _():
                    far_raw_copies[k][0][1].wait_recv()
                    turn_down(far_raw, 0)

            pl.when(ends)(far_large_copies[k][0][1].wait_recv)
            receives = jnp.where(is_last[k], place[k] > 1, receives)

        @pl.when(receives)
        def _():
            path_copies[k][0][1].wait_recv()

        @pl.when(jnp.logical_not(receives))
        def _():
            inbox[k] = jnp.zeros(inbox.shape[1:], jnp.float32)

        for v in range(nv):
            packed = inbox[k, v // group]
            shift = (v % group) * width
            paths[k, 0, v] = pltpu.roll(packed, LANES - shift, 1) if shift else packed

        def load(at):
            return [paths[k, at, v] for v in range(nv)]

        def store(at, state):
            for v in range(nv):
                paths[k, at, v] = state[v]

        def step(line, state):
            capped = large_lines[k, pl.ds(line, SUBLANES, stride=0), :]
            under = jnp.where(sub == 0, FAR, pltpu.roll(state[-1], 1, 0))
            over = jnp.where(sub == SUBLANES - 1, FAR, pltpu.roll(state[0], SUBLANES - 1, 0))
            beside = []
            for v in range(nv):
                low = state[v - 1] if v else under
                high = state[v + 1] if v < nv - 1 else over
                beside.append(jnp.minimum(low, high))
            if nv % 4 == 0:
                lowest = tree_min([beside[v] for v in range(nv) if v % 4 in (1, 2)])
            else:
                lowest = tree_min(state)
            lowest = all_sublanes_min(lowest)
            capped = capped + lowest
            fresh = []
            for v in range(nv):
                near = jnp.minimum(state[v], beside[v] + small)
                fresh.append(step_costs[line, v] + jnp.minimum(near, capped))
            return fresh, lowest

        def early(index, carry):
            state = load(0)
            for part in range(UNROLL):
                at = index * UNROLL + part
                if backward[k]:
                    at = jnp.where(at < span, span - 1 - at, 3 * span - 1 - at)
                state, _ = step(at, state)
            store(0, state)
            return carry

        def late(index, carry):
            state = load(index * UNROLL)
            for part in range(UNROLL):
                at = index * UNROLL + part
                line = length - 1 - at if backward[k] else at
                state, lowest = step(span + (own_base if axis == 0 else 0) + line, state)
                store(at + 1, state)
                lowests[k, at] = lowest
            return carry

        begin = jnp.where(ends, 0, span // UNROLL) if SKIPS[k] else span // UNROLL
        end = span // UNROLL
        if axis == 0:
            end = jnp.where(hands_on[k], (span + length) // UNROLL, end)
        lax.fori_loop(begin, end, early, 0)
        lax.fori_loop(0, length // UNROLL, late, 0)

        after = places[k] - 1 - place[k]

        @pl.when(both(hands_on[k], after >= (2 if SKIPS[k] else 1)))
        def _():
            above = lowests[k, length - 1]
            sent = [part - above for part in load(length)]
            for slot in range(nv // group):
                packed = sent[slot * group]
                for g in range(1, group):
                    moved = pltpu.roll(sent[slot * group + g], g * width, 1)
                    packed = jnp.where(lane >= g * width, moved, packed)
                outbox[k, slot] = packed

        start(path_copies[k])

    def total(axis):
        k = 2 * axis
        width = lines[k]
        group = LANES // width

        def some(index, carry):
            packed = [None] * nv
            for j in range(group):
                line = index * group + j
                back = lengths[k] - 1 - line
                above = lowests[k, line] + lowests[k + 1, back]
                for v in range(nv):
                    part = paths[k, line + 1, v] + paths[k + 1, back + 1, v] - above
                    if j:
                        part = jnp.where(lane >= j * width, pltpu.roll(part, j * width, 1), packed[v])
                    packed[v] = part
            for h in range(halves):
                per = LANES // SUBLANES
                turned = jnp.concatenate(packed[h * per : (h + 1) * per], axis=0).T
                if axis == 0:
                    for j in range(group):
                        at = pl.ds(index * group + j, width, stride=cols)
                        totals[axis, h, at, :] = turned[j * width : (j + 1) * width]
                else:
                    at = pl.ds(index * LANES, LANES)
                    totals[axis, h, at, :] = turned
            return carry

        for index in range(rows * cols // LANES):
            some(index, None)

    turns = max(nz, ny)
    down_done = jnp.maximum(place[2], place[3])
    turn_left = jnp.where(places[1] - 1 - place[1] >= 2, place[1], turns)
    ends_left = both(is_last[1], place[1] > 0)

    def one_turn(turn_at, carry):
        @pl.when(both(turn_at == turns - 1, ends_left))
        def _():
            forward_copies[1][0][1].wait_recv()
            for c in range(CORES):
                turn_across(far_across.at[c], c * cols)

        pl.when(turn_at == turn_left)(lambda: task(1))
        pl.when(both(turn_at == 0, iz == nz - 1))(lambda: turn_down(own_raw, rows))
        pl.when(turn_at == place[2])(lambda: task(2))
        pl.when(turn_at == place[3])(lambda: task(3))
        pl.when(both(turn_at == 0, iz < nz - 1))(take_mate)

        @pl.when(both(turn_at == turns - 2, ends_left))
        def _():
            far_raw_copies[1][0][1].wait_recv()
            start(forward_copies[1])

        pl.when(turn_at == down_done)(lambda: total(1))
        pl.when(turn_at == place[0])(lambda: task(0))
        return carry

    lax.fori_loop(0, turns + 1, one_turn, 0)
    total(0)
    rest = jnp.concatenate([totals[0, h] + totals[1, h] for h in range(halves)], axis=1)
    rest = rest * OUT_SCALE
    result = None
    for part in range(3):
        piece = rest.astype(jnp.bfloat16)
        moved = lax.dot_general(
            piece, order[...], (((1,), (0,)), ((), ())), preferred_element_type=jnp.float32
        )
        result = moved if part == 0 else result + moved
        if part < 2:
            rest = rest - piece.astype(jnp.float32)
    out_ref[...] = result

    drain(mate_copies)
    pl.when(ends_left)(forward_copies[1][0][1].wait_send)
    for k in range(4):
        drain(edge_copies[k])
        drain(path_copies[k])
        drain(far_raw_copies[k])
        drain(far_large_copies[k])


def on_device(cost_volume, left_image, p_small, p_large):
    rows, cols, disparities = cost_volume.shape
    nv = disparities // SUBLANES
    longest = max(rows, cols)
    packed = nv * longest // LANES
    halves = disparities // LANES
    block = (halves, rows * cols, LANES)
    hbm = pl.BlockSpec(memory_space=pltpu.HBM)
    vmem = pl.BlockSpec(memory_space=pltpu.VMEM)
    total = pl.pallas_call(
        functools.partial(kernel, rows, cols),
        out_shape=jax.ShapeDtypeStruct((rows * cols, disparities), jnp.float32),
        in_specs=[hbm] * 4,
        out_specs=vmem,
        scratch_shapes=[
            pltpu.SMEM((4,), jnp.int32),
            pltpu.SMEM((4,), jnp.int32),
            pltpu.VMEM((rows, cols), jnp.float32),
            pltpu.VMEM((rows, cols), jnp.float32),
            pltpu.VMEM(block, jnp.int32),
            pltpu.VMEM(block, jnp.int32),
            pltpu.VMEM(block, jnp.int32),
            pltpu.VMEM((CORES, *block), jnp.int32),
            pltpu.VMEM((disparities, disparities), jnp.bfloat16),
            pltpu.VMEM((2, halves, rows * cols, LANES), jnp.float32),
            pltpu.VMEM((2 * CORES * cols, nv, SUBLANES, LANES), jnp.float32),
            pltpu.VMEM((2 * rows, nv, SUBLANES, LANES), jnp.float32),
            pltpu.VMEM((4, longest + 1, nv, SUBLANES, LANES), jnp.float32),
            pltpu.VMEM((4, longest, SUBLANES, LANES), jnp.float32),
            pltpu.VMEM((4, 2 * CORES * longest, LANES), jnp.float32),
            pltpu.VMEM((2, CORES * longest, LANES), jnp.float32),
            pltpu.VMEM((4, packed, SUBLANES, LANES), jnp.float32),
            pltpu.VMEM((4, packed, SUBLANES, LANES), jnp.float32),
            pltpu.VMEM((4, SUBLANES, LANES), jnp.float32),
            pltpu.VMEM((4, SUBLANES, LANES), jnp.float32),
            pltpu.SemaphoreType.DMA((SENDS,)),
            pltpu.SemaphoreType.DMA((20,)),
            pltpu.SemaphoreType.DMA((3 + halves,)),
        ],
        compiler_params=pltpu.CompilerParams(
            collective_id=0, has_side_effects=True, vmem_limit_bytes=VMEM_BYTES
        ),
    )(
        *(
            pltpu.with_memory_space_constraint(array, pltpu.HBM)
            for array in (
                cost_volume.reshape(rows * cols, disparities),
                left_image,
                p_small,
                p_large,
            )
        )
    )
    return total.reshape(rows, cols, disparities)


def solution(mesh):
    in_specs = (P("gy", "gx", None), P("gy", "gx"), P(), P())
    out_specs = P("gy", "gx", None)
    return jax.shard_map(
        on_device, mesh=mesh, in_specs=in_specs, out_specs=out_specs, check_vma=False
    )
```

```python
import functools

import jax
import jax.numpy as jnp
from jax import lax
from jax.experimental import pallas as pl
from jax.experimental.pallas import tpu as pltpu
from jax.sharding import PartitionSpec as P

FAR = 1e30
GRADIENT_GAIN = 4.0
OUT_SCALE = 1.0 / 256.0
LANES = 128
SUBLANES = 8
UNROLL = 2
CORES = 2
SENDS = 30
VMEM_BYTES = 40 << 20
SKIPS = (False, True, True, True)
MESH = pl.DeviceIdType.MESH


def tree_min(parts):
    parts = list(parts)
    while len(parts) > 1:
        pairs = [jnp.minimum(a, b) for a, b in zip(parts[::2], parts[1::2])]
        parts = pairs + ([parts[-1]] if len(parts) % 2 else [])
    return parts[0]


def all_sublanes_min(x):
    for by in (4, 2, 1):
        x = jnp.minimum(x, pltpu.roll(x, by, 0))
    return x


def kernel(
    rows,
    cols,
    cost_hbm,
    image_hbm,
    small_hbm,
    large_hbm,
    out_ref,
    small_ref,
    large_ref,
    own_image,
    mate_image,
    own_raw,
    mate_raw,
    far_raw,
    far_across,
    order,
    totals,
    across_costs,
    down_costs,
    paths,
    lowests,
    large_lines,
    image_lines,
    outbox,
    inbox,
    edge_out,
    edge_in,
    send_sems,
    recv_sems,
    local_sems,
):
    disparities = cost_hbm.shape[1]
    nv = disparities // SUBLANES
    halves = disparities // LANES
    nx, ny = lax.axis_size("gx"), lax.axis_size("gy")
    ix, iy = lax.axis_index("gx"), lax.axis_index("gy")
    nz = nx // CORES
    iz, core = ix // CORES, ix % CORES
    mate = {"gx": iz * CORES + 1 - core}
    own_base = core * cols
    spans = (CORES * cols, rows)
    costs = (across_costs, down_costs)
    lengths = (cols, cols, rows, rows)
    lines = (rows, rows, cols, cols)
    backward = (False, True, False, True)

    place = (iz, nz - 1 - iz, iy, ny - 1 - iy)
    places = (nz, nz, ny, ny)
    hands_on = (core == 1, core == 0, True, True)
    is_last = [place[k] == places[k] - 1 for k in range(4)]

    def next_across(k, by, to_core):
        step = -by if backward[k] else by
        return {"gx": (iz + step) * CORES + to_core}

    def next_down(k, by):
        return {"gy": iy - by if backward[k] else iy + by}

    def prev_across(k, by):
        return next_across(k, -by, 0 if backward[k] else 1)

    def both(*flags):
        result = True
        for flag in flags:
            result = flag if result is True else jnp.logical_and(result, flag)
        return result

    sends = iter(range(SENDS))

    def remote(source, target, recv, device):
        return pltpu.make_async_remote_copy(
            src_ref=source,
            dst_ref=target,
            send_sem=send_sems.at[next(sends)],
            recv_sem=recv_sems.at[recv],
            device_id=device,
            device_id_type=MESH,
        )

    mate_copies = [
        (None, remote(own_image, mate_image, 0, mate)),
        (None, remote(own_raw, mate_raw, 1, mate)),
    ]
    edge_copies, path_copies, far_raw_copies, far_large_copies = [], [], [], []
    forward_copies = {}
    for k in range(4):
        sent = hands_on[k]
        after = places[k] - 1 - place[k]
        near_end = 2 if SKIPS[k] else 1
        if k < 2:
            to = lambda by, k=k: [next_across(k, by, c) for c in range(CORES)]
            same_core = next_across(k, 1, core)
        else:
            to = lambda by, k=k: [next_down(k, by)]
            same_core = next_down(k, 1)
        edge_copies.append(
            [
                (both(sent, after >= 1), remote(edge_out.at[k], edge_in.at[k], 2 + k, device))
                for device in to(1)
            ]
        )
        path_copies.append(
            [
                (both(sent, after >= near_end), remote(outbox.at[k], inbox.at[k], 6 + k, device))
                for device in to(1)
            ]
        )
        if SKIPS[k]:
            path_copies[k] += [
                (both(sent, after == 2), remote(outbox.at[k], inbox.at[k], 6 + k, device))
                for device in to(2)
            ]
            span = spans[k // 2]
            target = far_across.at[core] if k < 2 else far_raw
            far_raw_copies.append([(after == 1, remote(own_raw, target, 10 + k, same_core))])
            far_large_copies.append(
                [
                    (
                        after == 1,
                        remote(
                            large_lines.at[k, pl.ds(span, span)],
                            large_lines.at[k, pl.ds(0, span)],
                            14 + k,
                            same_core,
                        ),
                    )
                ]
            )
            if k < 2:
                here = far_across.at[core]
                forward_copies[k] = [(None, remote(here, here, 18 + k, mate))]
        else:
            far_raw_copies.append([])
            far_large_copies.append([])

    def start(copies):
        for flag, copy in copies:
            if flag is None:
                copy.start()
            else:
                pl.when(flag)(copy.start)

    def drain(copies):
        for flag, copy in copies:
            if flag is None:
                copy.wait_send()
            else:
                pl.when(flag)(copy.wait_send)

    locals_ = [
        pltpu.make_async_copy(source, target, local_sems.at[at])
        for at, (source, target) in enumerate(
            (
                (image_hbm, own_image),
                (small_hbm, small_ref),
                (large_hbm, large_ref),
                *(
                    (cost_hbm.at[:, pl.ds(h * LANES, LANES)], own_raw.at[h])
                    for h in range(halves)
                ),
            )
        )
    ]
    for copy in locals_:
        copy.start()

    barrier = pltpu.get_barrier_semaphore()

    def greet(device):
        pl.semaphore_signal(barrier, inc=1, device_id=device, device_id_type=MESH)

    greet(mate)
    awaited = jnp.int32(1)
    for k in range(4):
        after = places[k] - 1 - place[k]
        ends = both(after == 0, place[k] > 0)
        skips = both(after == 0, place[k] > 1)
        if k < 2:
            pl.when(place[k] > 0)(functools.partial(greet, prev_across(k, 1)))
            awaited += jnp.where(both(hands_on[k], after >= 1), CORES, 0)
            if SKIPS[k]:
                far_only = jnp.logical_not(hands_on[k])
                pl.when(both(ends, far_only))(
                    functools.partial(greet, next_across(k, -1, core))
                )
                awaited += jnp.where(both(far_only, after == 1), 1, 0)
                pl.when(skips)(functools.partial(greet, prev_across(k, 2)))
                awaited += jnp.where(both(hands_on[k], after == 2), CORES, 0)
        else:
            pl.when(place[k] > 0)(functools.partial(greet, next_down(k, -1)))
            awaited += jnp.where(after >= 1, 1, 0)
            if SKIPS[k]:
                pl.when(skips)(functools.partial(greet, next_down(k, -2)))
                awaited += jnp.where(after == 2, 1, 0)

    shape = (disparities, disparities)
    source = lax.broadcasted_iota(jnp.int32, shape, 1)
    target = lax.broadcasted_iota(jnp.int32, shape, 0)
    wanted = target // SUBLANES + nv * (target % SUBLANES)
    order[...] = jnp.where(source == wanted, 1.0, 0.0).astype(jnp.bfloat16)

    for copy in locals_[:3]:
        copy.wait()
    image = own_image[...]
    image_lines[...] = jnp.zeros_like(image_lines)
    image_lines[1, 0:rows, :cols] = image
    image_lines[0, pl.ds(pl.multiple_of(own_base, SUBLANES), cols), :rows] = image.T
    edge_out[...] = jnp.zeros_like(edge_out)
    edge_out[0, 0:1, :rows] = image.T[cols - 1 : cols, :]
    edge_out[1, 0:1, :rows] = image.T[0:1, :]
    edge_out[2, 0:1, :cols] = image[rows - 1 : rows, :]
    edge_out[3, 0:1, :cols] = image[0:1, :]
    for copy in locals_[3:]:
        copy.wait()

    def turn(origin, into, base, axis):
        width = lines[2 * axis]
        group = LANES // width

        def some(index, carry):
            first = index * group
            block = []
            for h in range(halves):
                if axis == 0:
                    parts = [
                        origin[h, pl.ds(first + j, width, stride=cols), :] for j in range(group)
                    ]
                    block.append(jnp.concatenate(parts, axis=0))
                else:
                    at = pl.ds(index * LANES, LANES)
                    block.append(origin[h, at, :])
            block = jnp.concatenate(block, axis=1).astype(jnp.float32).astype(jnp.bfloat16)
            block = lax.dot_general(
                order[...], block, (((1,), (1,)), ((), ())), preferred_element_type=jnp.float32
            )
            for j in range(group):
                moved = pltpu.roll(block, LANES - j * width, 1) if j else block
                into[base + first + j] = moved.reshape(nv, SUBLANES, LANES)
            return carry

        for index in range(rows * cols // LANES):
            some(index, None)

    def turn_across(origin, base):
        turn(origin, across_costs, base, 0)

    def turn_down(origin, base):
        turn(origin, down_costs, base, 1)

    def take_mate():
        for _, copy in mate_copies:
            copy.wait_recv()
        at = pl.ds(pl.multiple_of(cols - own_base, SUBLANES), cols)
        image_lines[0, at, :rows] = mate_image[...].T
        turn_across(mate_raw, spans[0] + cols - own_base)

    pl.semaphore_wait(barrier, awaited)
    start(mate_copies)
    for k in range(4):
        start(edge_copies[k])
    for k in range(4):
        start(far_raw_copies[k])

    pl.when(iz < nz - 1)(lambda: turn_down(own_raw, rows))
    turn_across(own_raw, spans[0] + own_base)
    pl.when(iz == nz - 1)(take_mate)

    sub = lax.broadcasted_iota(jnp.int32, (SUBLANES, LANES), 0)
    lane = lax.broadcasted_iota(jnp.int32, (SUBLANES, LANES), 1)

    def penalties(k):
        axis = k // 2
        small = small_ref[k].astype(jnp.float32)
        large = large_ref[k].astype(jnp.float32)
        span = spans[axis]
        own = image_lines[axis, :span, :]
        edge = edge_in[k, 0:1, :]
        if backward[k]:
            before = jnp.concatenate([own[1:], edge], axis=0)
        else:
            before = jnp.concatenate([edge, own[:-1]], axis=0)
        large_lines[k, span : 2 * span] = small + (large - small) / (
            1.0 + GRADIENT_GAIN * jnp.abs(own - before)
        )

    def early_penalties(k):
        edge_in[k] = jnp.zeros((SUBLANES, LANES), jnp.float32)
        penalties(k)
        start(far_large_copies[k])

    def later_penalties(k):
        edge_copies[k][0][1].wait_recv()
        penalties(k)
        start(far_large_copies[k])

    def task(k):
        axis = k // 2
        length, width = lengths[k], lines[k]
        group = LANES // width
        small = small_ref[k].astype(jnp.float32)
        step_costs = costs[axis]
        span = spans[axis]
        first = place[k] == 0
        pl.when(first)(lambda: early_penalties(k))
        ends = both(is_last[k], jnp.logical_not(first)) if SKIPS[k] else False
        receives = jnp.logical_not(first)
        if SKIPS[k]:
            if axis == 1:

                @pl.when(ends)
                def _():
                    far_raw_copies[k][0][1].wait_recv()
                    turn_down(far_raw, 0)

            pl.when(ends)(far_large_copies[k][0][1].wait_recv)
            receives = jnp.where(is_last[k], place[k] > 1, receives)

        @pl.when(receives)
        def _():
            path_copies[k][0][1].wait_recv()

        @pl.when(jnp.logical_not(receives))
        def _():
            inbox[k] = jnp.zeros(inbox.shape[1:], jnp.float32)

        for v in range(nv):
            packed = inbox[k, v // group]
            shift = (v % group) * width
            paths[k, 0, v] = pltpu.roll(packed, LANES - shift, 1) if shift else packed

        def load(at):
            return [paths[k, at, v] for v in range(nv)]

        def store(at, state):
            for v in range(nv):
                paths[k, at, v] = state[v]

        def step(line, state):
            capped = large_lines[k, pl.ds(line, SUBLANES, stride=0), :]
            under = jnp.where(sub == 0, FAR, pltpu.roll(state[-1], 1, 0))
            over = jnp.where(sub == SUBLANES - 1, FAR, pltpu.roll(state[0], SUBLANES - 1, 0))
            beside = []
            for v in range(nv):
                low = state[v - 1] if v else under
                high = state[v + 1] if v < nv - 1 else over
                beside.append(jnp.minimum(low, high))
            if nv % 4 == 0:
                lowest = tree_min([beside[v] for v in range(nv) if v % 4 in (1, 2)])
            else:
                lowest = tree_min(state)
            lowest = all_sublanes_min(lowest)
            capped = capped + lowest
            fresh = []
            for v in range(nv):
                near = jnp.minimum(state[v], beside[v] + small)
                fresh.append(step_costs[line, v] + jnp.minimum(near, capped))
            return fresh, lowest

        def early(index, carry):
            state = load(0)
            for part in range(UNROLL):
                at = index * UNROLL + part
                if backward[k]:
                    at = jnp.where(at < span, span - 1 - at, 3 * span - 1 - at)
                state, _ = step(at, state)
            store(0, state)
            return carry

        def late(index, carry):
            state = load(index * UNROLL)
            for part in range(UNROLL):
                at = index * UNROLL + part
                line = length - 1 - at if backward[k] else at
                state, lowest = step(span + (own_base if axis == 0 else 0) + line, state)
                store(at + 1, state)
                lowests[k, at] = lowest
            return carry

        begin = jnp.where(ends, 0, span // UNROLL) if SKIPS[k] else span // UNROLL
        end = span // UNROLL
        if axis == 0:
            end = jnp.where(hands_on[k], (span + length) // UNROLL, end)
        lax.fori_loop(begin, end, early, 0)
        lax.fori_loop(0, length // UNROLL, late, 0)

        after = places[k] - 1 - place[k]

        @pl.when(both(hands_on[k], after >= (2 if SKIPS[k] else 1)))
        def _():
            above = lowests[k, length - 1]
            sent = [part - above for part in load(length)]
            for slot in range(nv // group):
                packed = sent[slot * group]
                for g in range(1, group):
                    moved = pltpu.roll(sent[slot * group + g], g * width, 1)
                    packed = jnp.where(lane >= g * width, moved, packed)
                outbox[k, slot] = packed

        start(path_copies[k])

    def total(axis):
        k = 2 * axis
        width = lines[k]
        group = LANES // width

        def some(index, carry):
            packed = [None] * nv
            for j in range(group):
                line = index * group + j
                back = lengths[k] - 1 - line
                above = lowests[k, line] + lowests[k + 1, back]
                for v in range(nv):
                    part = paths[k, line + 1, v] + paths[k + 1, back + 1, v] - above
                    if j:
                        part = jnp.where(lane >= j * width, pltpu.roll(part, j * width, 1), packed[v])
                    packed[v] = part
            for h in range(halves):
                per = LANES // SUBLANES
                turned = jnp.concatenate(packed[h * per : (h + 1) * per], axis=0).T
                if axis == 0:
                    for j in range(group):
                        at = pl.ds(index * group + j, width, stride=cols)
                        totals[axis, h, at, :] = turned[j * width : (j + 1) * width]
                else:
                    at = pl.ds(index * LANES, LANES)
                    totals[axis, h, at, :] = turned
            return carry

        for index in range(rows * cols // LANES):
            some(index, None)

    turns = max(nz, ny)
    down_done = jnp.maximum(place[2], place[3])
    turn_left = jnp.where(places[1] - 1 - place[1] >= 2, place[1], turns)
    ends_left = both(is_last[1], place[1] > 0)

    def one_turn(turn_at, carry):
        @pl.when(both(turn_at == turns, ends_left))
        def _():
            forward_copies[1][0][1].wait_recv()
            for c in range(CORES):
                turn_across(far_across.at[c], c * cols)

        pl.when(turn_at == turn_left)(lambda: task(1))
        pl.when(both(turn_at == 0, iz == nz - 1))(lambda: turn_down(own_raw, rows))
        pl.when(turn_at == place[2])(lambda: task(2))
        pl.when(turn_at == place[3])(lambda: task(3))
        pl.when(both(turn_at == 0, iz < nz - 1))(take_mate)

        @pl.when(both(turn_at == turns - 2, ends_left))
        def _():
            far_raw_copies[1][0][1].wait_recv()
            start(forward_copies[1])

        pl.when(turn_at == down_done)(lambda: total(1))
        pl.when(turn_at == place[0])(lambda: task(0))

        @pl.when(turn_at == 0)
        def _():
            for k in range(4):
                pl.when(place[k] > 0)(functools.partial(later_penalties, k))

        return carry

    lax.fori_loop(0, turns + 1, one_turn, 0)
    total(0)
    rest = jnp.concatenate([totals[0, h] + totals[1, h] for h in range(halves)], axis=1)
    rest = rest * OUT_SCALE
    result = None
    for part in range(3):
        piece = rest.astype(jnp.bfloat16)
        moved = lax.dot_general(
            piece, order[...], (((1,), (0,)), ((), ())), preferred_element_type=jnp.float32
        )
        result = moved if part == 0 else result + moved
        if part < 2:
            rest = rest - piece.astype(jnp.float32)
    out_ref[...] = result

    drain(mate_copies)
    pl.when(ends_left)(forward_copies[1][0][1].wait_send)
    for k in range(4):
        drain(edge_copies[k])
        drain(path_copies[k])
        drain(far_raw_copies[k])
        drain(far_large_copies[k])


def on_device(cost_volume, left_image, p_small, p_large):
    rows, cols, disparities = cost_volume.shape
    nv = disparities // SUBLANES
    longest = max(rows, cols)
    packed = nv * longest // LANES
    halves = disparities // LANES
    block = (halves, rows * cols, LANES)
    hbm = pl.BlockSpec(memory_space=pltpu.HBM)
    vmem = pl.BlockSpec(memory_space=pltpu.VMEM)
    total = pl.pallas_call(
        functools.partial(kernel, rows, cols),
        out_shape=jax.ShapeDtypeStruct((rows * cols, disparities), jnp.float32),
        in_specs=[hbm] * 4,
        out_specs=vmem,
        scratch_shapes=[
            pltpu.SMEM((4,), jnp.int32),
            pltpu.SMEM((4,), jnp.int32),
            pltpu.VMEM((rows, cols), jnp.float32),
            pltpu.VMEM((rows, cols), jnp.float32),
            pltpu.VMEM(block, jnp.int32),
            pltpu.VMEM(block, jnp.int32),
            pltpu.VMEM(block, jnp.int32),
            pltpu.VMEM((CORES, *block), jnp.int32),
            pltpu.VMEM((disparities, disparities), jnp.bfloat16),
            pltpu.VMEM((2, halves, rows * cols, LANES), jnp.float32),
            pltpu.VMEM((2 * CORES * cols, nv, SUBLANES, LANES), jnp.float32),
            pltpu.VMEM((2 * rows, nv, SUBLANES, LANES), jnp.float32),
            pltpu.VMEM((4, longest + 1, nv, SUBLANES, LANES), jnp.float32),
            pltpu.VMEM((4, longest, SUBLANES, LANES), jnp.float32),
            pltpu.VMEM((4, 2 * CORES * longest, LANES), jnp.float32),
            pltpu.VMEM((2, CORES * longest, LANES), jnp.float32),
            pltpu.VMEM((4, packed, SUBLANES, LANES), jnp.float32),
            pltpu.VMEM((4, packed, SUBLANES, LANES), jnp.float32),
            pltpu.VMEM((4, SUBLANES, LANES), jnp.float32),
            pltpu.VMEM((4, SUBLANES, LANES), jnp.float32),
            pltpu.SemaphoreType.DMA((SENDS,)),
            pltpu.SemaphoreType.DMA((20,)),
            pltpu.SemaphoreType.DMA((3 + halves,)),
        ],
        compiler_params=pltpu.CompilerParams(
            collective_id=0, has_side_effects=True, vmem_limit_bytes=VMEM_BYTES
        ),
    )(
        *(
            pltpu.with_memory_space_constraint(array, pltpu.HBM)
            for array in (
                cost_volume.reshape(rows * cols, disparities),
                left_image,
                p_small,
                p_large,
            )
        )
    )
    return total.reshape(rows, cols, disparities)


def solution(mesh):
    in_specs = (P("gy", "gx", None), P("gy", "gx"), P(), P())
    out_specs = P("gy", "gx", None)
    return jax.shard_map(
        on_device, mesh=mesh, in_specs=in_specs, out_specs=out_specs, check_vma=False
    )
```

```python
import functools

import jax
import jax.numpy as jnp
from jax import lax
from jax.experimental import pallas as pl
from jax.experimental.pallas import tpu as pltpu
from jax.sharding import PartitionSpec as P

FAR = 1e30
GRADIENT_GAIN = 4.0
OUT_SCALE = 1.0 / 256.0
LANES = 128
SUBLANES = 8
UNROLL = 2
CORES = 2
DIRECT = 4
SENDS = 30
VMEM_BYTES = 40 << 20
SKIPS = (False, True, True, True)
MESH = pl.DeviceIdType.MESH


def tree_min(parts):
    parts = list(parts)
    while len(parts) > 1:
        pairs = [jnp.minimum(a, b) for a, b in zip(parts[::2], parts[1::2])]
        parts = pairs + ([parts[-1]] if len(parts) % 2 else [])
    return parts[0]


def all_sublanes_min(x):
    for by in (4, 2, 1):
        x = jnp.minimum(x, pltpu.roll(x, by, 0))
    return x


def kernel(
    rows,
    cols,
    cost_hbm,
    image_hbm,
    small_hbm,
    large_hbm,
    out_ref,
    small_ref,
    large_ref,
    own_image,
    mate_image,
    own_raw,
    mate_raw,
    far_raw,
    far_across,
    turned,
    order,
    totals,
    across_costs,
    down_costs,
    paths,
    lowests,
    large_lines,
    image_lines,
    outbox,
    inbox,
    edge_out,
    edge_in,
    send_sems,
    recv_sems,
    local_sems,
):
    disparities = cost_hbm.shape[1]
    nv = disparities // SUBLANES
    halves = disparities // LANES
    nx, ny = lax.axis_size("gx"), lax.axis_size("gy")
    ix, iy = lax.axis_index("gx"), lax.axis_index("gy")
    nz = nx // CORES
    iz, core = ix // CORES, ix % CORES
    mate = {"gx": iz * CORES + 1 - core}
    own_base = core * cols
    spans = (CORES * cols, rows)
    costs = (across_costs, down_costs)
    lengths = (cols, cols, rows, rows)
    lines = (rows, rows, cols, cols)
    backward = (False, True, False, True)

    place = (iz, nz - 1 - iz, iy, ny - 1 - iy)
    places = (nz, nz, ny, ny)
    hands_on = (core == 1, core == 0, True, True)
    is_last = [place[k] == places[k] - 1 for k in range(4)]

    def next_across(k, by, to_core):
        step = -by if backward[k] else by
        return {"gx": (iz + step) * CORES + to_core}

    def next_down(k, by):
        return {"gy": iy - by if backward[k] else iy + by}

    def prev_across(k, by):
        return next_across(k, -by, 0 if backward[k] else 1)

    def both(*flags):
        result = True
        for flag in flags:
            result = flag if result is True else jnp.logical_and(result, flag)
        return result

    sends = iter(range(SENDS))

    def remote(source, target, recv, device):
        return pltpu.make_async_remote_copy(
            src_ref=source,
            dst_ref=target,
            send_sem=send_sems.at[next(sends)],
            recv_sem=recv_sems.at[recv],
            device_id=device,
            device_id_type=MESH,
        )

    mate_copies = [
        (None, remote(own_image, mate_image, 0, mate)),
        (None, remote(own_raw, mate_raw, 1, mate)),
    ]
    edge_copies, path_copies, far_raw_copies, far_large_copies = [], [], [], []
    forward_copies = {}
    for k in range(4):
        sent = hands_on[k]
        after = places[k] - 1 - place[k]
        near_end = 2 if SKIPS[k] else 1
        if k < 2:
            to = lambda by, k=k: [
                next_across(k, by, c) for c in ((0, 1) if backward[k] else (1, 0))
            ]
            same_core = next_across(k, 1, core)
        else:
            to = lambda by, k=k: [next_down(k, by)]
            same_core = next_down(k, 1)
        edge_copies.append(
            [
                (both(sent, after >= 1), remote(edge_out.at[k], edge_in.at[k], 2 + k, device))
                for device in to(1)
            ]
        )
        path_copies.append(
            [
                (both(sent, after >= near_end), remote(outbox.at[k], inbox.at[k], 6 + k, device))
                for device in to(1)
            ]
        )
        if SKIPS[k]:
            path_copies[k] = [
                (both(sent, after == 2), remote(outbox.at[k], inbox.at[k], 6 + k, device))
                for device in to(2)
            ] + path_copies[k]
            span = spans[k // 2]
            target = far_across.at[core] if k < 2 else far_raw
            far_raw_copies.append([(after == 1, remote(own_raw, target, 10 + k, same_core))])
            far_large_copies.append(
                [
                    (
                        after == 1,
                        remote(
                            large_lines.at[k, pl.ds(span, span)],
                            large_lines.at[k, pl.ds(0, span)],
                            14 + k,
                            same_core,
                        ),
                    )
                ]
            )
            if k < 2:
                here = far_across.at[core]
                forward_copies[k] = [(None, remote(here, here, 18 + k, mate))]
        else:
            far_raw_copies.append([])
            far_large_copies.append([])

    def start(copies):
        for flag, copy in copies:
            if flag is None:
                copy.start()
            else:
                pl.when(flag)(copy.start)

    def drain(copies):
        for flag, copy in copies:
            if flag is None:
                copy.wait_send()
            else:
                pl.when(flag)(copy.wait_send)

    locals_ = [
        pltpu.make_async_copy(source, target, local_sems.at[at])
        for at, (source, target) in enumerate(
            (
                (image_hbm, own_image),
                (small_hbm, small_ref),
                (large_hbm, large_ref),
                *(
                    (cost_hbm.at[:, pl.ds(h * LANES, LANES)], own_raw.at[h])
                    for h in range(halves)
                ),
            )
        )
    ]
    for copy in locals_:
        copy.start()

    barrier = pltpu.get_barrier_semaphore()

    def greet(device):
        pl.semaphore_signal(barrier, inc=1, device_id=device, device_id_type=MESH)

    greet(mate)
    awaited = jnp.int32(1)
    for k in range(4):
        after = places[k] - 1 - place[k]
        ends = both(after == 0, place[k] > 0)
        skips = both(after == 0, place[k] > 1)
        if k < 2:
            pl.when(place[k] > 0)(functools.partial(greet, prev_across(k, 1)))
            awaited += jnp.where(both(hands_on[k], after >= 1), CORES, 0)
            if SKIPS[k]:
                far_only = jnp.logical_not(hands_on[k])
                pl.when(both(ends, far_only))(
                    functools.partial(greet, next_across(k, -1, core))
                )
                awaited += jnp.where(both(far_only, after == 1), 1, 0)
                pl.when(skips)(functools.partial(greet, prev_across(k, 2)))
                awaited += jnp.where(both(hands_on[k], after == 2), CORES, 0)
        else:
            pl.when(place[k] > 0)(functools.partial(greet, next_down(k, -1)))
            awaited += jnp.where(after >= 1, 1, 0)
            if SKIPS[k]:
                pl.when(skips)(functools.partial(greet, next_down(k, -2)))
                awaited += jnp.where(after == 2, 1, 0)

    for copy in locals_[:3]:
        copy.wait()
    image = own_image[...]
    image_lines[...] = jnp.zeros_like(image_lines)
    image_lines[1, 0:rows, :cols] = image
    image_lines[0, pl.ds(pl.multiple_of(own_base, SUBLANES), cols), :rows] = image.T
    edge_out[...] = jnp.zeros_like(edge_out)
    edge_out[0, 0:1, :rows] = image.T[cols - 1 : cols, :]
    edge_out[1, 0:1, :rows] = image.T[0:1, :]
    edge_out[2, 0:1, :cols] = image[rows - 1 : rows, :]
    edge_out[3, 0:1, :cols] = image[0:1, :]

    def turn(origin, into, base, axis):
        width = lines[2 * axis]
        group = LANES // width

        def some(index, carry):
            first = index * group
            block = []
            for h in range(halves):
                if axis == 0:
                    parts = [
                        origin[h, pl.ds(first + j, width, stride=cols), :] for j in range(group)
                    ]
                    block.append(jnp.concatenate(parts, axis=0))
                else:
                    at = pl.ds(index * LANES, LANES)
                    block.append(origin[h, at, :])
            block = jnp.concatenate(block, axis=1).astype(jnp.float32).astype(jnp.bfloat16)
            def product(part):
                return lax.dot_general(
                    order[...], part, (((1,), (1,)), ((), ())), preferred_element_type=jnp.float32
                )

            whole = product(block)
            for j in range(group):
                if j >= group - DIRECT:
                    alone = product(block[j * width : (j + 1) * width])
                    into[base + first + j, :, :, :width] = alone.reshape(nv, SUBLANES, width)
                else:
                    moved = pltpu.roll(whole, LANES - j * width, 1) if j else whole
                    into[base + first + j] = moved.reshape(nv, SUBLANES, LANES)
            return carry

        for index in range(rows * cols // LANES):
            some(index, None)

    def turn_across(origin, base):
        turn(origin, across_costs, base, 0)

    def turn_down(origin, base):
        turn(origin, down_costs, base, 1)

    def take_mate():
        for _, copy in mate_copies:
            copy.wait_recv()
        at = pl.ds(pl.multiple_of(cols - own_base, SUBLANES), cols)
        image_lines[0, at, :rows] = mate_image[...].T
        turn_across(mate_raw, spans[0] + cols)

    pl.semaphore_wait(barrier, awaited)
    start(mate_copies[:1])
    for k in range(4):
        start(edge_copies[k])
    for copy in locals_[3:]:
        copy.wait()
    start(mate_copies[1:])
    for k in range(4):
        start(far_raw_copies[k])

    shape = (disparities, disparities)
    source = lax.broadcasted_iota(jnp.int32, shape, 1)
    target = lax.broadcasted_iota(jnp.int32, shape, 0)
    wanted = target // SUBLANES + nv * (target % SUBLANES)
    order[...] = jnp.where(source == wanted, 1.0, 0.0).astype(jnp.bfloat16)


    pl.when(iz < nz - 1)(lambda: turn_down(own_raw, rows))
    turn_across(own_raw, spans[0])
    pl.when(iz == nz - 1)(take_mate)

    sub = lax.broadcasted_iota(jnp.int32, (SUBLANES, LANES), 0)
    lane = lax.broadcasted_iota(jnp.int32, (SUBLANES, LANES), 1)

    def penalties(k):
        axis = k // 2
        small = small_ref[k].astype(jnp.float32)
        large = large_ref[k].astype(jnp.float32)
        span = spans[axis]
        own = image_lines[axis, :span, :]
        edge = edge_in[k, 0:1, :]
        if backward[k]:
            before = jnp.concatenate([own[1:], edge], axis=0)
        else:
            before = jnp.concatenate([edge, own[:-1]], axis=0)
        large_lines[k, span : 2 * span] = small + (large - small) / (
            1.0 + GRADIENT_GAIN * jnp.abs(own - before)
        )

    def early_penalties(k):
        edge_in[k] = jnp.zeros((SUBLANES, LANES), jnp.float32)
        penalties(k)
        start(far_large_copies[k])

    def later_penalties(k):
        edge_copies[k][0][1].wait_recv()
        penalties(k)
        start(far_large_copies[k])

    def task(k):
        axis = k // 2
        length, width = lengths[k], lines[k]
        group = LANES // width
        small = small_ref[k].astype(jnp.float32)
        step_costs = costs[axis]
        span = spans[axis]
        first = place[k] == 0
        pl.when(first)(lambda: early_penalties(k))
        ends = both(is_last[k], jnp.logical_not(first)) if SKIPS[k] else False
        receives = jnp.logical_not(first)
        if SKIPS[k]:
            if axis == 1:

                @pl.when(ends)
                def _():
                    far_raw_copies[k][0][1].wait_recv()
                    turn_down(far_raw, 0)

            pl.when(ends)(far_large_copies[k][0][1].wait_recv)
            receives = jnp.where(is_last[k], place[k] > 1, receives)

        @pl.when(receives)
        def _():
            path_copies[k][0][1].wait_recv()

        @pl.when(jnp.logical_not(receives))
        def _():
            inbox[k] = jnp.zeros(inbox.shape[1:], jnp.float32)

        for v in range(nv):
            packed = inbox[k, v // group]
            shift = (v % group) * width
            paths[k, 0, v] = pltpu.roll(packed, LANES - shift, 1) if shift else packed

        def load(at):
            return [paths[k, at, v] for v in range(nv)]

        def store(at, state):
            for v in range(nv):
                paths[k, at, v] = state[v]

        def step(line, cost_line, state):
            capped = large_lines[k, pl.ds(line, SUBLANES, stride=0), :]
            under = jnp.where(sub == 0, FAR, pltpu.roll(state[-1], 1, 0))
            over = jnp.where(sub == SUBLANES - 1, FAR, pltpu.roll(state[0], SUBLANES - 1, 0))
            beside = []
            for v in range(nv):
                low = state[v - 1] if v else under
                high = state[v + 1] if v < nv - 1 else over
                beside.append(jnp.minimum(low, high))
            if nv % 4 == 0:
                lowest = tree_min([beside[v] for v in range(nv) if v % 4 in (1, 2)])
            else:
                lowest = tree_min(state)
            lowest = all_sublanes_min(lowest)
            capped = capped + lowest
            fresh = []
            for v in range(nv):
                near = jnp.minimum(state[v], beside[v] + small)
                fresh.append(step_costs[cost_line, v] + jnp.minimum(near, capped))
            return fresh, lowest

        def early(index, carry):
            state = load(0)
            for part in range(UNROLL):
                at = index * UNROLL + part
                if backward[k]:
                    at = jnp.where(at < span, span - 1 - at, 3 * span - 1 - at)
                cost_at = at
                if axis == 0:
                    cost_at = jnp.where(at < span, at, at + own_base)
                state, _ = step(at, cost_at, state)
            store(0, state)
            return carry

        def late(index, carry):
            state = load(index * UNROLL)
            for part in range(UNROLL):
                at = index * UNROLL + part
                line = length - 1 - at if backward[k] else at
                own_line = span + (own_base if axis == 0 else 0) + line
                state, lowest = step(own_line, span + line, state)
                store(at + 1, state)
                lowests[k, at] = lowest
            return carry

        begin = jnp.where(ends, 0, span // UNROLL) if SKIPS[k] else span // UNROLL
        end = span // UNROLL
        if axis == 0:
            end = jnp.where(hands_on[k], (span + length) // UNROLL, end)
        lax.fori_loop(begin, end, early, 0)
        lax.fori_loop(0, length // UNROLL, late, 0)

        after = places[k] - 1 - place[k]

        @pl.when(both(hands_on[k], after >= (2 if SKIPS[k] else 1)))
        def _():
            above = lowests[k, length - 1]
            sent = [part - above for part in load(length)]
            for slot in range(nv // group):
                packed = sent[slot * group]
                for g in range(1, group):
                    moved = pltpu.roll(sent[slot * group + g], g * width, 1)
                    packed = jnp.where(lane >= g * width, moved, packed)
                outbox[k, slot] = packed

        start(path_copies[k])

    def total(axis):
        k = 2 * axis
        width = lines[k]
        group = LANES // width

        def some(index):
            for j in range(group):
                line = index * group + j
                back = lengths[k] - 1 - line
                above = lowests[k, line] + lowests[k + 1, back]
                parts = [above] + [
                    paths[k, line + 1, v] + paths[k + 1, back + 1, v] for v in range(nv)
                ]
                if j:
                    parts = [
                        jnp.where(lane >= j * width, pltpu.roll(part, j * width, 1), before)
                        for part, before in zip(parts, packed)
                    ]
                packed = parts
            packed = [part - packed[0] for part in packed[1:]]
            for v in range(nv):
                turned[index, pl.ds(v, SUBLANES, stride=nv), :] = packed[v]
            for h in range(halves):
                block = turned[index, h * LANES : (h + 1) * LANES].T
                if axis == 0:
                    for j in range(group):
                        at = pl.ds(index * group + j, width, stride=cols)
                        totals[axis, h, at, :] = block[j * width : (j + 1) * width]
                else:
                    totals[axis, h, pl.ds(index * LANES, LANES), :] = block

        for index in range(rows * cols // LANES):
            some(index)

    turns = max(nz, ny)
    turn_down_at = [
        jnp.where(places[k] - 1 - place[k] == 1, place[k] + 1, place[k]) if SKIPS[k] else place[k]
        for k in (2, 3)
    ]
    down_done = jnp.maximum(*turn_down_at)
    turn_left = jnp.where(places[1] - 1 - place[1] >= 2, place[1], turns)
    ends_left = both(is_last[1], place[1] > 0)

    def one_turn(turn_at, carry):
        @pl.when(both(turn_at == turns, ends_left))
        def _():
            forward_copies[1][0][1].wait_recv()
            for c in range(CORES):
                turn_across(far_across.at[c], c * cols)

        pl.when(turn_at == turn_left)(lambda: task(1))
        pl.when(both(turn_at == 0, iz == nz - 1))(lambda: turn_down(own_raw, rows))
        pl.when(turn_at == turn_down_at[0])(lambda: task(2))
        pl.when(turn_at == turn_down_at[1])(lambda: task(3))
        pl.when(both(turn_at == 0, iz < nz - 1))(take_mate)

        @pl.when(both(turn_at == turns - 2, ends_left))
        def _():
            far_raw_copies[1][0][1].wait_recv()
            start(forward_copies[1])

        pl.when(turn_at == down_done)(lambda: total(1))
        pl.when(turn_at == place[0])(lambda: task(0))

        @pl.when(turn_at == 0)
        def _():
            for k in range(4):
                pl.when(place[k] > 0)(functools.partial(later_penalties, k))

        return carry

    lax.fori_loop(0, turns + 1, one_turn, 0)
    total(0)
    for h in range(halves):
        out_ref[:, h * LANES : (h + 1) * LANES] = (totals[0, h] + totals[1, h]) * OUT_SCALE

    drain(mate_copies)
    pl.when(ends_left)(forward_copies[1][0][1].wait_send)
    for k in range(4):
        drain(edge_copies[k])
        drain(path_copies[k])
        drain(far_raw_copies[k])
        drain(far_large_copies[k])


def on_device(cost_volume, left_image, p_small, p_large):
    rows, cols, disparities = cost_volume.shape
    nv = disparities // SUBLANES
    longest = max(rows, cols)
    packed = nv * longest // LANES
    halves = disparities // LANES
    block = (halves, rows * cols, LANES)
    hbm = pl.BlockSpec(memory_space=pltpu.HBM)
    vmem = pl.BlockSpec(memory_space=pltpu.VMEM)
    total = pl.pallas_call(
        functools.partial(kernel, rows, cols),
        out_shape=jax.ShapeDtypeStruct((rows * cols, disparities), jnp.float32),
        in_specs=[hbm] * 4,
        out_specs=vmem,
        scratch_shapes=[
            pltpu.SMEM((4,), jnp.int32),
            pltpu.SMEM((4,), jnp.int32),
            pltpu.VMEM((rows, cols), jnp.float32),
            pltpu.VMEM((rows, cols), jnp.float32),
            pltpu.VMEM(block, jnp.int32),
            pltpu.VMEM(block, jnp.int32),
            pltpu.VMEM(block, jnp.int32),
            pltpu.VMEM((CORES, *block), jnp.int32),
            pltpu.VMEM((rows * cols // LANES, disparities, LANES), jnp.float32),
            pltpu.VMEM((disparities, disparities), jnp.bfloat16),
            pltpu.VMEM((2, halves, rows * cols, LANES), jnp.float32),
            pltpu.VMEM((2 * CORES * cols, nv, SUBLANES, LANES), jnp.float32),
            pltpu.VMEM((2 * rows, nv, SUBLANES, LANES), jnp.float32),
            pltpu.VMEM((4, longest + 1, nv, SUBLANES, LANES), jnp.float32),
            pltpu.VMEM((4, longest, SUBLANES, LANES), jnp.float32),
            pltpu.VMEM((4, 2 * CORES * longest, LANES), jnp.float32),
            pltpu.VMEM((2, CORES * longest, LANES), jnp.float32),
            pltpu.VMEM((4, packed, SUBLANES, LANES), jnp.float32),
            pltpu.VMEM((4, packed, SUBLANES, LANES), jnp.float32),
            pltpu.VMEM((4, SUBLANES, LANES), jnp.float32),
            pltpu.VMEM((4, SUBLANES, LANES), jnp.float32),
            pltpu.SemaphoreType.DMA((SENDS,)),
            pltpu.SemaphoreType.DMA((20,)),
            pltpu.SemaphoreType.DMA((3 + halves,)),
        ],
        compiler_params=pltpu.CompilerParams(
            collective_id=0,
            has_side_effects=True,
            vmem_limit_bytes=VMEM_BYTES,
        ),
    )(
        *(
            pltpu.with_memory_space_constraint(array, pltpu.HBM)
            for array in (
                cost_volume.reshape(rows * cols, disparities),
                left_image,
                p_small,
                p_large,
            )
        )
    )
    return total.reshape(rows, cols, disparities)


def solution(mesh):
    in_specs = (P("gy", "gx", None), P("gy", "gx"), P(), P())
    out_specs = P("gy", "gx", None)
    return jax.shard_map(
        on_device, mesh=mesh, in_specs=in_specs, out_specs=out_specs, check_vma=False
    )
```

```python
import functools

import jax
import jax.numpy as jnp
from jax import lax
from jax.experimental import pallas as pl
from jax.experimental.pallas import tpu as pltpu
from jax.sharding import PartitionSpec as P

FAR = 1e30
GRADIENT_GAIN = 4.0
OUT_SCALE = 1.0 / 256.0
LANES = 128
SUBLANES = 8
UNROLL = 2
CORES = 2
DIRECT = 4
SENDS = 30
VMEM_BYTES = 40 << 20
SKIPS = (False, True, True, True)
MESH = pl.DeviceIdType.MESH


def tree_min(parts):
    parts = list(parts)
    while len(parts) > 1:
        pairs = [jnp.minimum(a, b) for a, b in zip(parts[::2], parts[1::2])]
        parts = pairs + ([parts[-1]] if len(parts) % 2 else [])
    return parts[0]


def all_sublanes_min(x):
    for by in (4, 2, 1):
        x = jnp.minimum(x, pltpu.roll(x, by, 0))
    return x


def kernel(
    rows,
    cols,
    cost_hbm,
    image_hbm,
    small_hbm,
    large_hbm,
    out_ref,
    small_ref,
    large_ref,
    own_image,
    mate_image,
    own_raw,
    mate_raw,
    far_raw,
    far_across,
    turned,
    order,
    totals,
    across_costs,
    down_costs,
    paths,
    lowests,
    large_lines,
    image_lines,
    outbox,
    inbox,
    edge_out,
    edge_in,
    send_sems,
    recv_sems,
    local_sems,
):
    disparities = cost_hbm.shape[1]
    nv = disparities // SUBLANES
    halves = disparities // LANES
    nx, ny = lax.axis_size("gx"), lax.axis_size("gy")
    ix, iy = lax.axis_index("gx"), lax.axis_index("gy")
    nz = nx // CORES
    iz, core = ix // CORES, ix % CORES
    mate = {"gx": iz * CORES + 1 - core}
    own_base = core * cols
    spans = (CORES * cols, rows)
    costs = (across_costs, down_costs)
    lengths = (cols, cols, rows, rows)
    lines = (rows, rows, cols, cols)
    backward = (False, True, False, True)

    place = (iz, nz - 1 - iz, iy, ny - 1 - iy)
    places = (nz, nz, ny, ny)
    hands_on = (core == 1, core == 0, True, True)
    is_last = [place[k] == places[k] - 1 for k in range(4)]

    def next_across(k, by, to_core):
        step = -by if backward[k] else by
        return {"gx": (iz + step) * CORES + to_core}

    def next_down(k, by):
        return {"gy": iy - by if backward[k] else iy + by}

    def prev_across(k, by):
        return next_across(k, -by, 0 if backward[k] else 1)

    def both(*flags):
        result = True
        for flag in flags:
            result = flag if result is True else jnp.logical_and(result, flag)
        return result

    sends = iter(range(SENDS))

    def remote(source, target, recv, device):
        return pltpu.make_async_remote_copy(
            src_ref=source,
            dst_ref=target,
            send_sem=send_sems.at[next(sends)],
            recv_sem=recv_sems.at[recv],
            device_id=device,
            device_id_type=MESH,
        )

    mate_copies = [
        (None, remote(own_image, mate_image, 0, mate)),
        (None, remote(own_raw, mate_raw, 1, mate)),
    ]
    edge_copies, path_copies, far_raw_copies, far_large_copies = [], [], [], []
    forward_copies = {}
    for k in range(4):
        sent = hands_on[k]
        after = places[k] - 1 - place[k]
        near_end = 2 if SKIPS[k] else 1
        if k < 2:
            to = lambda by, k=k: [
                next_across(k, by, c) for c in ((0, 1) if backward[k] else (1, 0))
            ]
            same_core = next_across(k, 1, core)
        else:
            to = lambda by, k=k: [next_down(k, by)]
            same_core = next_down(k, 1)
        edge_copies.append(
            [
                (both(sent, after >= 1), remote(edge_out.at[k], edge_in.at[k], 2 + k, device))
                for device in to(1)
            ]
        )
        path_copies.append(
            [
                (both(sent, after >= near_end), remote(outbox.at[k], inbox.at[k], 6 + k, device))
                for device in to(1)
            ]
        )
        if SKIPS[k]:
            path_copies[k] = [
                (both(sent, after == 2), remote(outbox.at[k], inbox.at[k], 6 + k, device))
                for device in to(2)
            ] + path_copies[k]
            span = spans[k // 2]
            target = far_across.at[core] if k < 2 else far_raw
            far_raw_copies.append([(after == 1, remote(own_raw, target, 10 + k, same_core))])
            far_large_copies.append(
                [
                    (
                        after == 1,
                        remote(
                            large_lines.at[k, pl.ds(span, span)],
                            large_lines.at[k, pl.ds(0, span)],
                            14 + k,
                            same_core,
                        ),
                    )
                ]
            )
            if k < 2:
                here = far_across.at[core]
                forward_copies[k] = [(None, remote(here, here, 18 + k, mate))]
        else:
            far_raw_copies.append([])
            far_large_copies.append([])

    def start(copies):
        for flag, copy in copies:
            if flag is None:
                copy.start()
            else:
                pl.when(flag)(copy.start)

    def drain(copies):
        for flag, copy in copies:
            if flag is None:
                copy.wait_send()
            else:
                pl.when(flag)(copy.wait_send)

    locals_ = [
        pltpu.make_async_copy(source, target, local_sems.at[at])
        for at, (source, target) in enumerate(
            (
                (image_hbm, own_image),
                (small_hbm, small_ref),
                (large_hbm, large_ref),
                *(
                    (cost_hbm.at[:, pl.ds(h * LANES, LANES)], own_raw.at[h])
                    for h in range(halves)
                ),
            )
        )
    ]
    for copy in locals_:
        copy.start()

    barrier = pltpu.get_barrier_semaphore()

    def greet(device):
        pl.semaphore_signal(barrier, inc=1, device_id=device, device_id_type=MESH)

    greet(mate)
    awaited = jnp.int32(1)
    for k in range(4):
        after = places[k] - 1 - place[k]
        ends = both(after == 0, place[k] > 0)
        skips = both(after == 0, place[k] > 1)
        if k < 2:
            pl.when(place[k] > 0)(functools.partial(greet, prev_across(k, 1)))
            awaited += jnp.where(both(hands_on[k], after >= 1), CORES, 0)
            if SKIPS[k]:
                far_only = jnp.logical_not(hands_on[k])
                pl.when(both(ends, far_only))(
                    functools.partial(greet, next_across(k, -1, core))
                )
                awaited += jnp.where(both(far_only, after == 1), 1, 0)
                pl.when(skips)(functools.partial(greet, prev_across(k, 2)))
                awaited += jnp.where(both(hands_on[k], after == 2), CORES, 0)
        else:
            pl.when(place[k] > 0)(functools.partial(greet, next_down(k, -1)))
            awaited += jnp.where(after >= 1, 1, 0)
            if SKIPS[k]:
                pl.when(skips)(functools.partial(greet, next_down(k, -2)))
                awaited += jnp.where(after == 2, 1, 0)

    for copy in locals_[:3]:
        copy.wait()
    image = own_image[...]
    image_lines[...] = jnp.zeros_like(image_lines)
    image_lines[1, 0:rows, :cols] = image
    image_lines[0, pl.ds(pl.multiple_of(own_base, SUBLANES), cols), :rows] = image.T
    edge_out[...] = jnp.zeros_like(edge_out)
    edge_out[0, 0:1, :rows] = image.T[cols - 1 : cols, :]
    edge_out[1, 0:1, :rows] = image.T[0:1, :]
    edge_out[2, 0:1, :cols] = image[rows - 1 : rows, :]
    edge_out[3, 0:1, :cols] = image[0:1, :]

    def turn(origin, into, base, axis):
        width = lines[2 * axis]
        group = LANES // width

        def some(index, carry):
            first = index * group
            block = []
            for h in range(halves):
                if axis == 0:
                    parts = [
                        origin[h, pl.ds(first + j, width, stride=cols), :] for j in range(group)
                    ]
                    block.append(jnp.concatenate(parts, axis=0))
                else:
                    at = pl.ds(index * LANES, LANES)
                    block.append(origin[h, at, :])
            block = jnp.concatenate(block, axis=1).astype(jnp.float32).astype(jnp.bfloat16)
            def product(part):
                return lax.dot_general(
                    order[...], part, (((1,), (1,)), ((), ())), preferred_element_type=jnp.float32
                )

            whole = product(block)
            for j in range(group):
                if j >= group - DIRECT:
                    alone = product(block[j * width : (j + 1) * width])
                    into[base + first + j, :, :, :width] = alone.reshape(nv, SUBLANES, width)
                else:
                    moved = pltpu.roll(whole, LANES - j * width, 1) if j else whole
                    into[base + first + j] = moved.reshape(nv, SUBLANES, LANES)
            return carry

        for index in range(rows * cols // LANES):
            some(index, None)

    def turn_across(origin, base):
        turn(origin, across_costs, base, 0)

    def turn_down(origin, base):
        turn(origin, down_costs, base, 1)

    def take_mate():
        for _, copy in mate_copies:
            copy.wait_recv()
        at = pl.ds(pl.multiple_of(cols - own_base, SUBLANES), cols)
        image_lines[0, at, :rows] = mate_image[...].T
        turn_across(mate_raw, spans[0] + cols)

    pl.semaphore_wait(barrier, awaited)
    start(mate_copies[:1])
    for k in range(4):
        start(edge_copies[k])
    for copy in locals_[3:]:
        copy.wait()
    start(mate_copies[1:])

    def start_far():
        for k in range(4):
            start(far_raw_copies[k])

    pl.when(core == 0)(start_far)

    shape = (disparities, disparities)
    source = lax.broadcasted_iota(jnp.int32, shape, 1)
    target = lax.broadcasted_iota(jnp.int32, shape, 0)
    wanted = target // SUBLANES + nv * (target % SUBLANES)
    order[...] = jnp.where(source == wanted, 1.0, 0.0).astype(jnp.bfloat16)


    pl.when(iz < nz - 1)(lambda: turn_down(own_raw, rows))
    turn_across(own_raw, spans[0])
    pl.when(iz == nz - 1)(take_mate)

    sub = lax.broadcasted_iota(jnp.int32, (SUBLANES, LANES), 0)
    lane = lax.broadcasted_iota(jnp.int32, (SUBLANES, LANES), 1)

    def penalties(k):
        axis = k // 2
        small = small_ref[k].astype(jnp.float32)
        large = large_ref[k].astype(jnp.float32)
        span = spans[axis]
        own = image_lines[axis, :span, :]
        edge = edge_in[k, 0:1, :]
        if backward[k]:
            before = jnp.concatenate([own[1:], edge], axis=0)
        else:
            before = jnp.concatenate([edge, own[:-1]], axis=0)
        large_lines[k, span : 2 * span] = small + (large - small) / (
            1.0 + GRADIENT_GAIN * jnp.abs(own - before)
        )

    def early_penalties(k):
        edge_in[k] = jnp.zeros((SUBLANES, LANES), jnp.float32)
        penalties(k)
        start(far_large_copies[k])

    def later_penalties(k):
        edge_copies[k][0][1].wait_recv()
        penalties(k)
        start(far_large_copies[k])

    def task(k):
        axis = k // 2
        length, width = lengths[k], lines[k]
        group = LANES // width
        small = small_ref[k].astype(jnp.float32)
        step_costs = costs[axis]
        span = spans[axis]
        first = place[k] == 0
        pl.when(first)(lambda: early_penalties(k))
        ends = both(is_last[k], jnp.logical_not(first)) if SKIPS[k] else False
        receives = jnp.logical_not(first)
        if SKIPS[k]:
            pl.when(ends)(far_large_copies[k][0][1].wait_recv)
            receives = jnp.where(is_last[k], place[k] > 1, receives)

        @pl.when(receives)
        def _():
            path_copies[k][0][1].wait_recv()

        @pl.when(jnp.logical_not(receives))
        def _():
            inbox[k] = jnp.zeros(inbox.shape[1:], jnp.float32)

        for v in range(nv):
            packed = inbox[k, v // group]
            shift = (v % group) * width
            paths[k, 0, v] = pltpu.roll(packed, LANES - shift, 1) if shift else packed

        def load(at):
            return [paths[k, at, v] for v in range(nv)]

        def store(at, state):
            for v in range(nv):
                paths[k, at, v] = state[v]

        def step(line, cost_line, state):
            capped = large_lines[k, pl.ds(line, SUBLANES, stride=0), :]
            under = jnp.where(sub == 0, FAR, pltpu.roll(state[-1], 1, 0))
            over = jnp.where(sub == SUBLANES - 1, FAR, pltpu.roll(state[0], SUBLANES - 1, 0))
            beside = []
            for v in range(nv):
                low = state[v - 1] if v else under
                high = state[v + 1] if v < nv - 1 else over
                beside.append(jnp.minimum(low, high))
            if nv % 4 == 0:
                lowest = tree_min([beside[v] for v in range(nv) if v % 4 in (1, 2)])
            else:
                lowest = tree_min(state)
            lowest = all_sublanes_min(lowest)
            capped = capped + lowest
            fresh = []
            for v in range(nv):
                near = jnp.minimum(state[v], beside[v] + small)
                fresh.append(step_costs[cost_line, v] + jnp.minimum(near, capped))
            return fresh, lowest

        def early(index, carry):
            state = load(0)
            for part in range(UNROLL):
                at = index * UNROLL + part
                if backward[k]:
                    at = jnp.where(at < span, span - 1 - at, 3 * span - 1 - at)
                cost_at = at
                if axis == 0:
                    cost_at = jnp.where(at < span, at, at + own_base)
                state, _ = step(at, cost_at, state)
            store(0, state)
            return carry

        def late(index, carry):
            state = load(index * UNROLL)
            for part in range(UNROLL):
                at = index * UNROLL + part
                line = length - 1 - at if backward[k] else at
                own_line = span + (own_base if axis == 0 else 0) + line
                state, lowest = step(own_line, span + line, state)
                store(at + 1, state)
                lowests[k, at] = lowest
            return carry

        begin = jnp.where(ends, 0, span // UNROLL) if SKIPS[k] else span // UNROLL
        end = span // UNROLL
        if axis == 0:
            end = jnp.where(hands_on[k], (span + length) // UNROLL, end)
        lax.fori_loop(begin, end, early, 0)
        lax.fori_loop(0, length // UNROLL, late, 0)

        after = places[k] - 1 - place[k]

        @pl.when(both(hands_on[k], after >= (2 if SKIPS[k] else 1)))
        def _():
            above = lowests[k, length - 1]
            sent = [part - above for part in load(length)]
            for slot in range(nv // group):
                packed = sent[slot * group]
                for g in range(1, group):
                    moved = pltpu.roll(sent[slot * group + g], g * width, 1)
                    packed = jnp.where(lane >= g * width, moved, packed)
                outbox[k, slot] = packed

        start(path_copies[k])

    def total(axis):
        k = 2 * axis
        width = lines[k]
        group = LANES // width

        def some(index):
            for j in range(group):
                line = index * group + j
                back = lengths[k] - 1 - line
                above = lowests[k, line] + lowests[k + 1, back]
                parts = [above] + [
                    paths[k, line + 1, v] + paths[k + 1, back + 1, v] for v in range(nv)
                ]
                if j:
                    parts = [
                        jnp.where(lane >= j * width, pltpu.roll(part, j * width, 1), before)
                        for part, before in zip(parts, packed)
                    ]
                packed = parts
            packed = [part - packed[0] for part in packed[1:]]
            for v in range(nv):
                turned[index, pl.ds(v, SUBLANES, stride=nv), :] = packed[v]
            for h in range(halves):
                block = turned[index, h * LANES : (h + 1) * LANES].T
                if axis == 0:
                    for j in range(group):
                        at = pl.ds(index * group + j, width, stride=cols)
                        totals[axis, h, at, :] = block[j * width : (j + 1) * width]
                else:
                    totals[axis, h, pl.ds(index * LANES, LANES), :] = block

        for index in range(rows * cols // LANES):
            some(index)

    turns = max(nz, ny)
    turn_down_at = [
        jnp.where(places[k] - 1 - place[k] == 1, place[k] + 1, place[k]) if SKIPS[k] else place[k]
        for k in (2, 3)
    ]
    down_done = jnp.maximum(*turn_down_at)
    turn_left = jnp.where(places[1] - 1 - place[1] >= 2, place[1], turns)
    ends_left = both(is_last[1], place[1] > 0)

    def take_forward():
        forward_copies[1][0][1].wait_recv()
        turn_across(far_across.at[1 - core], cols - own_base)

    def one_turn(turn_at, carry):
        pl.when(both(turn_at == turns, ends_left, core == 0))(take_forward)
        pl.when(turn_at == turn_left)(lambda: task(1))
        pl.when(both(turn_at == 0, iz == nz - 1))(lambda: turn_down(own_raw, rows))
        pl.when(turn_at == turn_down_at[0])(lambda: task(2))
        pl.when(turn_at == turn_down_at[1])(lambda: task(3))
        pl.when(both(turn_at == 0, iz < nz - 1))(take_mate)
        pl.when(both(turn_at == 0, core != 0))(start_far)

        pl.when(turn_at == down_done)(lambda: total(1))
        pl.when(turn_at == place[0])(lambda: task(0))

        @pl.when(turn_at == 0)
        def _():
            for k in range(4):
                pl.when(place[k] > 0)(functools.partial(later_penalties, k))

        fetched = turn_at == max(turns - 3, 0)

        pl.when(both(fetched, ends_left, core != 0))(take_forward)

        @pl.when(both(fetched, ends_left))
        def _():
            far_raw_copies[1][0][1].wait_recv()
            start(forward_copies[1])
            turn_across(far_across.at[core], own_base)

        for k in (2, 3):

            @pl.when(both(fetched, is_last[k], place[k] > 0))
            def _(k=k):
                far_raw_copies[k][0][1].wait_recv()
                turn_down(far_raw, 0)

        return carry

    lax.fori_loop(0, turns + 1, one_turn, 0)
    total(0)
    for h in range(halves):
        out_ref[:, h * LANES : (h + 1) * LANES] = (totals[0, h] + totals[1, h]) * OUT_SCALE

    drain(mate_copies)
    pl.when(ends_left)(forward_copies[1][0][1].wait_send)
    for k in range(4):
        drain(edge_copies[k])
        drain(path_copies[k])
        drain(far_raw_copies[k])
        drain(far_large_copies[k])


def on_device(cost_volume, left_image, p_small, p_large):
    rows, cols, disparities = cost_volume.shape
    nv = disparities // SUBLANES
    longest = max(rows, cols)
    packed = nv * longest // LANES
    halves = disparities // LANES
    block = (halves, rows * cols, LANES)
    hbm = pl.BlockSpec(memory_space=pltpu.HBM)
    vmem = pl.BlockSpec(memory_space=pltpu.VMEM)
    total = pl.pallas_call(
        functools.partial(kernel, rows, cols),
        out_shape=jax.ShapeDtypeStruct((rows * cols, disparities), jnp.float32),
        in_specs=[hbm] * 4,
        out_specs=vmem,
        scratch_shapes=[
            pltpu.SMEM((4,), jnp.int32),
            pltpu.SMEM((4,), jnp.int32),
            pltpu.VMEM((rows, cols), jnp.float32),
            pltpu.VMEM((rows, cols), jnp.float32),
            pltpu.VMEM(block, jnp.int32),
            pltpu.VMEM(block, jnp.int32),
            pltpu.VMEM(block, jnp.int32),
            pltpu.VMEM((CORES, *block), jnp.int32),
            pltpu.VMEM((rows * cols // LANES, disparities, LANES), jnp.float32),
            pltpu.VMEM((disparities, disparities), jnp.bfloat16),
            pltpu.VMEM((2, halves, rows * cols, LANES), jnp.float32),
            pltpu.VMEM((2 * CORES * cols, nv, SUBLANES, LANES), jnp.float32),
            pltpu.VMEM((2 * rows, nv, SUBLANES, LANES), jnp.float32),
            pltpu.VMEM((4, longest + 1, nv, SUBLANES, LANES), jnp.float32),
            pltpu.VMEM((4, longest, SUBLANES, LANES), jnp.float32),
            pltpu.VMEM((4, 2 * CORES * longest, LANES), jnp.float32),
            pltpu.VMEM((2, CORES * longest, LANES), jnp.float32),
            pltpu.VMEM((4, packed, SUBLANES, LANES), jnp.float32),
            pltpu.VMEM((4, packed, SUBLANES, LANES), jnp.float32),
            pltpu.VMEM((4, SUBLANES, LANES), jnp.float32),
            pltpu.VMEM((4, SUBLANES, LANES), jnp.float32),
            pltpu.SemaphoreType.DMA((SENDS,)),
            pltpu.SemaphoreType.DMA((20,)),
            pltpu.SemaphoreType.DMA((3 + halves,)),
        ],
        compiler_params=pltpu.CompilerParams(
            collective_id=0,
            has_side_effects=True,
            vmem_limit_bytes=VMEM_BYTES,
        ),
    )(
        *(
            pltpu.with_memory_space_constraint(array, pltpu.HBM)
            for array in (
                cost_volume.reshape(rows * cols, disparities),
                left_image,
                p_small,
                p_large,
            )
        )
    )
    return total.reshape(rows, cols, disparities)


def solution(mesh):
    in_specs = (P("gy", "gx", None), P("gy", "gx"), P(), P())
    out_specs = P("gy", "gx", None)
    return jax.shard_map(
        on_device, mesh=mesh, in_specs=in_specs, out_specs=out_specs, check_vma=False
    )
```

```python
import functools

import jax
import jax.numpy as jnp
from jax import lax
from jax.experimental import pallas as pl
from jax.experimental.pallas import tpu as pltpu
from jax.sharding import PartitionSpec as P

FAR = 1e30
GRADIENT_GAIN = 4.0
OUT_SCALE = 1.0 / 256.0
LANES = 128
SUBLANES = 8
UNROLL = 2
CORES = 2
DIRECT = 4
SENDS = 30
VMEM_BYTES = 40 << 20
SKIPS = (False, True, True, True)
MESH = pl.DeviceIdType.MESH


def tree_min(parts):
    parts = list(parts)
    while len(parts) > 1:
        pairs = [jnp.minimum(a, b) for a, b in zip(parts[::2], parts[1::2])]
        parts = pairs + ([parts[-1]] if len(parts) % 2 else [])
    return parts[0]


def all_sublanes_min(x):
    for by in (4, 2, 1):
        x = jnp.minimum(x, pltpu.roll(x, by, 0))
    return x


def kernel(
    rows,
    cols,
    cost_hbm,
    image_hbm,
    small_hbm,
    large_hbm,
    out_ref,
    small_ref,
    large_ref,
    own_image,
    mate_image,
    own_raw,
    mate_raw,
    far_raw,
    far_across,
    turned,
    order,
    totals,
    across_costs,
    down_costs,
    paths,
    lowests,
    large_lines,
    image_lines,
    outbox,
    inbox,
    edge_out,
    edge_in,
    send_sems,
    recv_sems,
    local_sems,
):
    disparities = cost_hbm.shape[1]
    nv = disparities // SUBLANES
    halves = disparities // LANES
    nx, ny = lax.axis_size("gx"), lax.axis_size("gy")
    ix, iy = lax.axis_index("gx"), lax.axis_index("gy")
    nz = nx // CORES
    iz, core = ix // CORES, ix % CORES
    mate = {"gx": iz * CORES + 1 - core}
    own_base = core * cols
    spans = (CORES * cols, rows)
    costs = (across_costs, down_costs)
    lengths = (cols, cols, rows, rows)
    lines = (rows, rows, cols, cols)
    backward = (False, True, False, True)

    place = (iz, nz - 1 - iz, iy, ny - 1 - iy)
    places = (nz, nz, ny, ny)
    hands_on = (core == 1, core == 0, True, True)
    is_last = [place[k] == places[k] - 1 for k in range(4)]

    def next_across(k, by, to_core):
        step = -by if backward[k] else by
        return {"gx": (iz + step) * CORES + to_core}

    def next_down(k, by):
        return {"gy": iy - by if backward[k] else iy + by}

    def prev_across(k, by):
        return next_across(k, -by, 0 if backward[k] else 1)

    def both(*flags):
        result = True
        for flag in flags:
            result = flag if result is True else jnp.logical_and(result, flag)
        return result

    sends = iter(range(SENDS))

    def remote(source, target, recv, device):
        return pltpu.make_async_remote_copy(
            src_ref=source,
            dst_ref=target,
            send_sem=send_sems.at[next(sends)],
            recv_sem=recv_sems.at[recv],
            device_id=device,
            device_id_type=MESH,
        )

    mate_copies = [
        (None, remote(own_image, mate_image, 0, mate)),
        (None, remote(own_raw, mate_raw, 1, mate)),
    ]
    edge_copies, path_copies, far_raw_copies, far_large_copies = [], [], [], []
    forward_copies = {}
    for k in range(4):
        sent = hands_on[k]
        after = places[k] - 1 - place[k]
        near_end = 2 if SKIPS[k] else 1
        if k < 2:
            to = lambda by, k=k: [
                next_across(k, by, c) for c in ((0, 1) if backward[k] else (1, 0))
            ]
            same_core = next_across(k, 1, core)
        else:
            to = lambda by, k=k: [next_down(k, by)]
            same_core = next_down(k, 1)
        edge_copies.append(
            [
                (both(sent, after >= 1), remote(edge_out.at[k], edge_in.at[k], 2 + k, device))
                for device in to(1)
            ]
        )
        path_copies.append(
            [
                (both(sent, after >= near_end), remote(outbox.at[k], inbox.at[k], 6 + k, device))
                for device in to(1)
            ]
        )
        if SKIPS[k]:
            path_copies[k] = [
                (both(sent, after == 2), remote(outbox.at[k], inbox.at[k], 6 + k, device))
                for device in to(2)
            ] + path_copies[k]
            span = spans[k // 2]
            target = far_across.at[core] if k < 2 else far_raw
            far_raw_copies.append([(after == 1, remote(own_raw, target, 10 + k, same_core))])
            far_large_copies.append(
                [
                    (
                        after == 1,
                        remote(
                            large_lines.at[k, pl.ds(span, span)],
                            large_lines.at[k, pl.ds(0, span)],
                            14 + k,
                            same_core,
                        ),
                    )
                ]
            )
            if k < 2:
                here = far_across.at[core]
                forward_copies[k] = [(None, remote(here, here, 18 + k, mate))]
        else:
            far_raw_copies.append([])
            far_large_copies.append([])

    def start(copies):
        for flag, copy in copies:
            if flag is None:
                copy.start()
            else:
                pl.when(flag)(copy.start)

    def drain(copies):
        for flag, copy in copies:
            if flag is None:
                copy.wait_send()
            else:
                pl.when(flag)(copy.wait_send)

    locals_ = [
        pltpu.make_async_copy(source, target, local_sems.at[at])
        for at, (source, target) in enumerate(
            (
                (image_hbm, own_image),
                (small_hbm, small_ref),
                (large_hbm, large_ref),
                *(
                    (cost_hbm.at[:, pl.ds(h * LANES, LANES)], own_raw.at[h])
                    for h in range(halves)
                ),
            )
        )
    ]
    for copy in locals_:
        copy.start()

    barrier = pltpu.get_barrier_semaphore()

    def greet(device):
        pl.semaphore_signal(barrier, inc=1, device_id=device, device_id_type=MESH)

    greet(mate)
    awaited = jnp.int32(1)
    for k in range(4):
        after = places[k] - 1 - place[k]
        ends = both(after == 0, place[k] > 0)
        skips = both(after == 0, place[k] > 1)
        if k < 2:
            pl.when(place[k] > 0)(functools.partial(greet, prev_across(k, 1)))
            awaited += jnp.where(both(hands_on[k], after >= 1), CORES, 0)
            if SKIPS[k]:
                far_only = jnp.logical_not(hands_on[k])
                pl.when(both(ends, far_only))(
                    functools.partial(greet, next_across(k, -1, core))
                )
                awaited += jnp.where(both(far_only, after == 1), 1, 0)
                pl.when(skips)(functools.partial(greet, prev_across(k, 2)))
                awaited += jnp.where(both(hands_on[k], after == 2), CORES, 0)
        else:
            pl.when(place[k] > 0)(functools.partial(greet, next_down(k, -1)))
            awaited += jnp.where(after >= 1, 1, 0)
            if SKIPS[k]:
                pl.when(skips)(functools.partial(greet, next_down(k, -2)))
                awaited += jnp.where(after == 2, 1, 0)

    for copy in locals_[:3]:
        copy.wait()
    image = own_image[...]
    image_lines[...] = jnp.zeros_like(image_lines)
    image_lines[1, 0:rows, :cols] = image
    image_lines[0, pl.ds(pl.multiple_of(own_base, SUBLANES), cols), :rows] = image.T
    edge_out[...] = jnp.zeros_like(edge_out)
    edge_out[0, 0:1, :rows] = image.T[cols - 1 : cols, :]
    edge_out[1, 0:1, :rows] = image.T[0:1, :]
    edge_out[2, 0:1, :cols] = image[rows - 1 : rows, :]
    edge_out[3, 0:1, :cols] = image[0:1, :]

    def turn(origin, into, base, axis):
        width = lines[2 * axis]
        group = LANES // width

        def some(index, carry):
            first = index * group
            block = []
            for h in range(halves):
                if axis == 0:
                    parts = [
                        origin[h, pl.ds(first + j, width, stride=cols), :] for j in range(group)
                    ]
                    block.append(jnp.concatenate(parts, axis=0))
                else:
                    at = pl.ds(index * LANES, LANES)
                    block.append(origin[h, at, :])
            block = jnp.concatenate(block, axis=1).astype(jnp.float32).astype(jnp.bfloat16)
            def product(part):
                return lax.dot_general(
                    order[...], part, (((1,), (1,)), ((), ())), preferred_element_type=jnp.float32
                )

            whole = product(block)
            for j in range(group):
                if j >= group - DIRECT:
                    alone = product(block[j * width : (j + 1) * width])
                    into[base + first + j, :, :, :width] = alone.reshape(nv, SUBLANES, width)
                else:
                    moved = pltpu.roll(whole, LANES - j * width, 1) if j else whole
                    into[base + first + j] = moved.reshape(nv, SUBLANES, LANES)
            return carry

        for index in range(rows * cols // LANES):
            some(index, None)

    def turn_across(origin, base):
        turn(origin, across_costs, base, 0)

    def turn_down(origin, base):
        turn(origin, down_costs, base, 1)

    def take_mate():
        for _, copy in mate_copies:
            copy.wait_recv()
        at = pl.ds(pl.multiple_of(cols - own_base, SUBLANES), cols)
        image_lines[0, at, :rows] = mate_image[...].T
        turn_across(mate_raw, spans[0] + cols)

    pl.semaphore_wait(barrier, awaited)
    start(mate_copies[:1])
    for k in range(4):
        start(edge_copies[k])
    for copy in locals_[3:]:
        copy.wait()

    def start_far():
        for k in range(4):
            start(far_raw_copies[k])

    at_start = iz == nz - 1
    pl.when(at_start)(mate_copies[1][1].start)
    pl.when(core == 0)(start_far)
    pl.when(jnp.logical_not(at_start))(mate_copies[1][1].start)

    shape = (disparities, disparities)
    source = lax.broadcasted_iota(jnp.int32, shape, 1)
    target = lax.broadcasted_iota(jnp.int32, shape, 0)
    wanted = target // SUBLANES + nv * (target % SUBLANES)
    order[...] = jnp.where(source == wanted, 1.0, 0.0).astype(jnp.bfloat16)


    pl.when(iz < nz - 1)(lambda: turn_down(own_raw, rows))
    turn_across(own_raw, spans[0])
    pl.when(iz == nz - 1)(take_mate)

    sub = lax.broadcasted_iota(jnp.int32, (SUBLANES, LANES), 0)
    lane = lax.broadcasted_iota(jnp.int32, (SUBLANES, LANES), 1)

    def penalties(k):
        axis = k // 2
        small = small_ref[k].astype(jnp.float32)
        large = large_ref[k].astype(jnp.float32)
        span = spans[axis]
        own = image_lines[axis, :span, :]
        edge = edge_in[k, 0:1, :]
        if backward[k]:
            before = jnp.concatenate([own[1:], edge], axis=0)
        else:
            before = jnp.concatenate([edge, own[:-1]], axis=0)
        large_lines[k, span : 2 * span] = small + (large - small) / (
            1.0 + GRADIENT_GAIN * jnp.abs(own - before)
        )

    def early_penalties(k):
        edge_in[k] = jnp.zeros((SUBLANES, LANES), jnp.float32)
        penalties(k)
        start(far_large_copies[k])

    def later_penalties(k):
        edge_copies[k][0][1].wait_recv()
        penalties(k)
        start(far_large_copies[k])

    def task(k):
        axis = k // 2
        length, width = lengths[k], lines[k]
        group = LANES // width
        small = small_ref[k].astype(jnp.float32)
        step_costs = costs[axis]
        span = spans[axis]
        first = place[k] == 0
        pl.when(first)(lambda: early_penalties(k))
        ends = both(is_last[k], jnp.logical_not(first)) if SKIPS[k] else False
        receives = jnp.logical_not(first)
        if SKIPS[k]:
            pl.when(ends)(far_large_copies[k][0][1].wait_recv)
            receives = jnp.where(is_last[k], place[k] > 1, receives)

        @pl.when(receives)
        def _():
            path_copies[k][0][1].wait_recv()

        @pl.when(jnp.logical_not(receives))
        def _():
            inbox[k] = jnp.zeros(inbox.shape[1:], jnp.float32)

        for v in range(nv):
            packed = inbox[k, v // group]
            shift = (v % group) * width
            paths[k, 0, v] = pltpu.roll(packed, LANES - shift, 1) if shift else packed

        def load(at):
            return [paths[k, at, v] for v in range(nv)]

        def store(at, state):
            for v in range(nv):
                paths[k, at, v] = state[v]

        def step(line, cost_line, state):
            capped = large_lines[k, pl.ds(line, SUBLANES, stride=0), :]
            under = jnp.where(sub == 0, FAR, pltpu.roll(state[-1], 1, 0))
            over = jnp.where(sub == SUBLANES - 1, FAR, pltpu.roll(state[0], SUBLANES - 1, 0))
            beside = []
            for v in range(nv):
                low = state[v - 1] if v else under
                high = state[v + 1] if v < nv - 1 else over
                beside.append(jnp.minimum(low, high))
            if nv % 4 == 0:
                lowest = tree_min([beside[v] for v in range(nv) if v % 4 in (1, 2)])
            else:
                lowest = tree_min(state)
            lowest = all_sublanes_min(lowest)
            capped = capped + lowest
            fresh = []
            for v in range(nv):
                near = jnp.minimum(state[v], beside[v] + small)
                fresh.append(step_costs[cost_line, v] + jnp.minimum(near, capped))
            return fresh, lowest

        def early(index, carry):
            state = load(0)
            for part in range(UNROLL):
                at = index * UNROLL + part
                if backward[k]:
                    at = jnp.where(at < span, span - 1 - at, 3 * span - 1 - at)
                cost_at = at
                if axis == 0:
                    cost_at = jnp.where(at < span, at, at + own_base)
                state, _ = step(at, cost_at, state)
            store(0, state)
            return carry

        def late(index, carry):
            state = load(index * UNROLL)
            for part in range(UNROLL):
                at = index * UNROLL + part
                line = length - 1 - at if backward[k] else at
                own_line = span + (own_base if axis == 0 else 0) + line
                state, lowest = step(own_line, span + line, state)
                store(at + 1, state)
                lowests[k, at] = lowest
            return carry

        begin = jnp.where(ends, 0, span // UNROLL) if SKIPS[k] else span // UNROLL
        end = span // UNROLL
        if axis == 0:
            end = jnp.where(hands_on[k], (span + length) // UNROLL, end)
        lax.fori_loop(begin, end, early, 0)
        lax.fori_loop(0, length // UNROLL, late, 0)

        after = places[k] - 1 - place[k]

        @pl.when(both(hands_on[k], after >= (2 if SKIPS[k] else 1)))
        def _():
            above = lowests[k, length - 1]
            sent = [part - above for part in load(length)]
            for slot in range(nv // group):
                packed = sent[slot * group]
                for g in range(1, group):
                    moved = pltpu.roll(sent[slot * group + g], g * width, 1)
                    packed = jnp.where(lane >= g * width, moved, packed)
                outbox[k, slot] = packed

        start(path_copies[k])

    def total(axis):
        k = 2 * axis
        width = lines[k]
        group = LANES // width

        def some(index):
            for j in range(group):
                line = index * group + j
                back = lengths[k] - 1 - line
                above = lowests[k, line] + lowests[k + 1, back]
                parts = [above] + [
                    paths[k, line + 1, v] + paths[k + 1, back + 1, v] for v in range(nv)
                ]
                if j:
                    parts = [
                        jnp.where(lane >= j * width, pltpu.roll(part, j * width, 1), before)
                        for part, before in zip(parts, packed)
                    ]
                packed = parts
            packed = [part - packed[0] for part in packed[1:]]
            for v in range(nv):
                turned[index, pl.ds(v, SUBLANES, stride=nv), :] = packed[v]
            for h in range(halves):
                block = turned[index, h * LANES : (h + 1) * LANES].T
                if axis == 0:
                    for j in range(group):
                        at = pl.ds(index * group + j, width, stride=cols)
                        totals[axis, h, at, :] = block[j * width : (j + 1) * width]
                else:
                    totals[axis, h, pl.ds(index * LANES, LANES), :] = block

        for index in range(rows * cols // LANES):
            some(index)

    turns = max(nz, ny)
    turn_down_at = [
        jnp.where(places[k] - 1 - place[k] == 1, place[k] + 1, place[k]) if SKIPS[k] else place[k]
        for k in (2, 3)
    ]
    down_done = jnp.maximum(*turn_down_at)
    turn_left = jnp.where(places[1] - 1 - place[1] >= 2, place[1], turns)
    ends_left = both(is_last[1], place[1] > 0)

    def take_forward():
        forward_copies[1][0][1].wait_recv()
        turn_across(far_across.at[1 - core], cols - own_base)

    def one_turn(turn_at, carry):
        pl.when(both(turn_at == turns, ends_left, core == 0))(take_forward)
        pl.when(turn_at == turn_left)(lambda: task(1))
        pl.when(both(turn_at == 0, iz == nz - 1))(lambda: turn_down(own_raw, rows))
        pl.when(turn_at == turn_down_at[0])(lambda: task(2))
        pl.when(turn_at == turn_down_at[1])(lambda: task(3))
        pl.when(both(turn_at == 0, iz < nz - 1))(take_mate)
        pl.when(both(turn_at == 0, core != 0))(start_far)

        pl.when(turn_at == down_done)(lambda: total(1))
        pl.when(turn_at == place[0])(lambda: task(0))

        @pl.when(turn_at == 0)
        def _():
            for k in range(4):
                pl.when(place[k] > 0)(functools.partial(later_penalties, k))

        fetched = turn_at == max(turns - 3, 0)

        pl.when(both(fetched, ends_left, core != 0))(take_forward)

        @pl.when(both(fetched, ends_left))
        def _():
            far_raw_copies[1][0][1].wait_recv()
            start(forward_copies[1])
            turn_across(far_across.at[core], own_base)

        for k in (2, 3):

            @pl.when(both(fetched, is_last[k], place[k] > 0))
            def _(k=k):
                far_raw_copies[k][0][1].wait_recv()
                turn_down(far_raw, 0)

        return carry

    lax.fori_loop(0, turns + 1, one_turn, 0)
    total(0)
    for h in range(halves):
        out_ref[:, h * LANES : (h + 1) * LANES] = (totals[0, h] + totals[1, h]) * OUT_SCALE

    drain(mate_copies)
    pl.when(ends_left)(forward_copies[1][0][1].wait_send)
    for k in range(4):
        drain(edge_copies[k])
        drain(path_copies[k])
        drain(far_raw_copies[k])
        drain(far_large_copies[k])


def on_device(cost_volume, left_image, p_small, p_large):
    rows, cols, disparities = cost_volume.shape
    nv = disparities // SUBLANES
    longest = max(rows, cols)
    packed = nv * longest // LANES
    halves = disparities // LANES
    block = (halves, rows * cols, LANES)
    hbm = pl.BlockSpec(memory_space=pltpu.HBM)
    vmem = pl.BlockSpec(memory_space=pltpu.VMEM)
    total = pl.pallas_call(
        functools.partial(kernel, rows, cols),
        out_shape=jax.ShapeDtypeStruct((rows * cols, disparities), jnp.float32),
        in_specs=[hbm] * 4,
        out_specs=vmem,
        scratch_shapes=[
            pltpu.SMEM((4,), jnp.int32),
            pltpu.SMEM((4,), jnp.int32),
            pltpu.VMEM((rows, cols), jnp.float32),
            pltpu.VMEM((rows, cols), jnp.float32),
            pltpu.VMEM(block, jnp.int32),
            pltpu.VMEM(block, jnp.int32),
            pltpu.VMEM(block, jnp.int32),
            pltpu.VMEM((CORES, *block), jnp.int32),
            pltpu.VMEM((rows * cols // LANES, disparities, LANES), jnp.float32),
            pltpu.VMEM((disparities, disparities), jnp.bfloat16),
            pltpu.VMEM((2, halves, rows * cols, LANES), jnp.float32),
            pltpu.VMEM((2 * CORES * cols, nv, SUBLANES, LANES), jnp.float32),
            pltpu.VMEM((2 * rows, nv, SUBLANES, LANES), jnp.float32),
            pltpu.VMEM((4, longest + 1, nv, SUBLANES, LANES), jnp.float32),
            pltpu.VMEM((4, longest, SUBLANES, LANES), jnp.float32),
            pltpu.VMEM((4, 2 * CORES * longest, LANES), jnp.float32),
            pltpu.VMEM((2, CORES * longest, LANES), jnp.float32),
            pltpu.VMEM((4, packed, SUBLANES, LANES), jnp.float32),
            pltpu.VMEM((4, packed, SUBLANES, LANES), jnp.float32),
            pltpu.VMEM((4, SUBLANES, LANES), jnp.float32),
            pltpu.VMEM((4, SUBLANES, LANES), jnp.float32),
            pltpu.SemaphoreType.DMA((SENDS,)),
            pltpu.SemaphoreType.DMA((20,)),
            pltpu.SemaphoreType.DMA((3 + halves,)),
        ],
        compiler_params=pltpu.CompilerParams(
            collective_id=0,
            has_side_effects=True,
            vmem_limit_bytes=VMEM_BYTES,
        ),
    )(
        *(
            pltpu.with_memory_space_constraint(array, pltpu.HBM)
            for array in (
                cost_volume.reshape(rows * cols, disparities),
                left_image,
                p_small,
                p_large,
            )
        )
    )
    return total.reshape(rows, cols, disparities)


def solution(mesh):
    in_specs = (P("gy", "gx", None), P("gy", "gx"), P(), P())
    out_specs = P("gy", "gx", None)
    return jax.shard_map(
        on_device, mesh=mesh, in_specs=in_specs, out_specs=out_specs, check_vma=False
    )
```

```python
import functools

import jax
import jax.numpy as jnp
from jax import lax
from jax.experimental import pallas as pl
from jax.experimental.pallas import tpu as pltpu
from jax.sharding import PartitionSpec as P

FAR = 1e30
GRADIENT_GAIN = 4.0
OUT_SCALE = 1.0 / 256.0
LANES = 128
SUBLANES = 8
UNROLL = 2
CORES = 2
DIRECT = 3
SENDS = 30
VMEM_BYTES = 40 << 20
SKIPS = (False, True, True, True)
MESH = pl.DeviceIdType.MESH


def tree_min(parts):
    parts = list(parts)
    while len(parts) > 1:
        pairs = [jnp.minimum(a, b) for a, b in zip(parts[::2], parts[1::2])]
        parts = pairs + ([parts[-1]] if len(parts) % 2 else [])
    return parts[0]


def all_sublanes_min(x):
    for by in (4, 2, 1):
        x = jnp.minimum(x, pltpu.roll(x, by, 0))
    return x


def kernel(
    rows,
    cols,
    cost_hbm,
    image_hbm,
    small_hbm,
    large_hbm,
    out_ref,
    small_ref,
    large_ref,
    own_image,
    mate_image,
    own_raw,
    mate_raw,
    far_raw,
    far_across,
    turned,
    order,
    totals,
    across_costs,
    down_costs,
    paths,
    lowests,
    large_lines,
    image_lines,
    outbox,
    inbox,
    edge_out,
    edge_in,
    send_sems,
    recv_sems,
    local_sems,
):
    disparities = cost_hbm.shape[1]
    nv = disparities // SUBLANES
    halves = disparities // LANES
    nx, ny = lax.axis_size("gx"), lax.axis_size("gy")
    ix, iy = lax.axis_index("gx"), lax.axis_index("gy")
    nz = nx // CORES
    iz, core = ix // CORES, ix % CORES
    mate = {"gx": iz * CORES + 1 - core}
    own_base = core * cols
    spans = (CORES * cols, rows)
    costs = (across_costs, down_costs)
    lengths = (cols, cols, rows, rows)
    lines = (rows, rows, cols, cols)
    backward = (False, True, False, True)

    place = (iz, nz - 1 - iz, iy, ny - 1 - iy)
    places = (nz, nz, ny, ny)
    hands_on = (core == 1, core == 0, True, True)
    is_last = [place[k] == places[k] - 1 for k in range(4)]

    def next_across(k, by, to_core):
        step = -by if backward[k] else by
        return {"gx": (iz + step) * CORES + to_core}

    def next_down(k, by):
        return {"gy": iy - by if backward[k] else iy + by}

    def prev_across(k, by):
        return next_across(k, -by, 0 if backward[k] else 1)

    def both(*flags):
        result = True
        for flag in flags:
            result = flag if result is True else jnp.logical_and(result, flag)
        return result

    sends = iter(range(SENDS))

    def remote(source, target, recv, device):
        return pltpu.make_async_remote_copy(
            src_ref=source,
            dst_ref=target,
            send_sem=send_sems.at[next(sends)],
            recv_sem=recv_sems.at[recv],
            device_id=device,
            device_id_type=MESH,
        )

    mate_copies = [
        (None, remote(own_image, mate_image, 0, mate)),
        (None, remote(own_raw, mate_raw, 1, mate)),
    ]
    edge_copies, path_copies, far_raw_copies, far_large_copies = [], [], [], []
    forward_copies = {}
    for k in range(4):
        sent = hands_on[k]
        after = places[k] - 1 - place[k]
        near_end = 2 if SKIPS[k] else 1
        if k < 2:
            to = lambda by, k=k: [
                next_across(k, by, c) for c in ((0, 1) if backward[k] else (1, 0))
            ]
            same_core = next_across(k, 1, core)
        else:
            to = lambda by, k=k: [next_down(k, by)]
            same_core = next_down(k, 1)
        edge_copies.append(
            [
                (both(sent, after >= 1), remote(edge_out.at[k], edge_in.at[k], 2 + k, device))
                for device in to(1)
            ]
        )
        path_copies.append(
            [
                (both(sent, after >= near_end), remote(outbox.at[k], inbox.at[k], 6 + k, device))
                for device in to(1)
            ]
        )
        if SKIPS[k]:
            path_copies[k] = [
                (both(sent, after == 2), remote(outbox.at[k], inbox.at[k], 6 + k, device))
                for device in to(2)
            ] + path_copies[k]
            span = spans[k // 2]
            target = far_across.at[core] if k < 2 else far_raw
            far_raw_copies.append([(after == 1, remote(own_raw, target, 10 + k, same_core))])
            far_large_copies.append(
                [
                    (
                        after == 1,
                        remote(
                            large_lines.at[k, pl.ds(span, span)],
                            large_lines.at[k, pl.ds(0, span)],
                            14 + k,
                            same_core,
                        ),
                    )
                ]
            )
            if k < 2:
                here = far_across.at[core]
                forward_copies[k] = [(None, remote(here, here, 18 + k, mate))]
        else:
            far_raw_copies.append([])
            far_large_copies.append([])

    def start(copies):
        for flag, copy in copies:
            if flag is None:
                copy.start()
            else:
                pl.when(flag)(copy.start)

    def drain(copies):
        for flag, copy in copies:
            if flag is None:
                copy.wait_send()
            else:
                pl.when(flag)(copy.wait_send)

    locals_ = [
        pltpu.make_async_copy(source, target, local_sems.at[at])
        for at, (source, target) in enumerate(
            (
                (image_hbm, own_image),
                (small_hbm, small_ref),
                (large_hbm, large_ref),
                *(
                    (cost_hbm.at[:, pl.ds(h * LANES, LANES)], own_raw.at[h])
                    for h in range(halves)
                ),
            )
        )
    ]
    for copy in locals_:
        copy.start()

    barrier = pltpu.get_barrier_semaphore()

    def greet(device):
        pl.semaphore_signal(barrier, inc=1, device_id=device, device_id_type=MESH)

    greet(mate)
    awaited = jnp.int32(1)
    for k in range(4):
        after = places[k] - 1 - place[k]
        ends = both(after == 0, place[k] > 0)
        skips = both(after == 0, place[k] > 1)
        if k < 2:
            pl.when(place[k] > 0)(functools.partial(greet, prev_across(k, 1)))
            awaited += jnp.where(both(hands_on[k], after >= 1), CORES, 0)
            if SKIPS[k]:
                far_only = jnp.logical_not(hands_on[k])
                pl.when(both(ends, far_only))(
                    functools.partial(greet, next_across(k, -1, core))
                )
                awaited += jnp.where(both(far_only, after == 1), 1, 0)
                pl.when(skips)(functools.partial(greet, prev_across(k, 2)))
                awaited += jnp.where(both(hands_on[k], after == 2), CORES, 0)
        else:
            pl.when(place[k] > 0)(functools.partial(greet, next_down(k, -1)))
            awaited += jnp.where(after >= 1, 1, 0)
            if SKIPS[k]:
                pl.when(skips)(functools.partial(greet, next_down(k, -2)))
                awaited += jnp.where(after == 2, 1, 0)

    for copy in locals_[:3]:
        copy.wait()
    image = own_image[...]
    image_lines[...] = jnp.zeros_like(image_lines)
    image_lines[1, 0:rows, :cols] = image
    image_lines[0, pl.ds(pl.multiple_of(own_base, SUBLANES), cols), :rows] = image.T
    edge_out[...] = jnp.zeros_like(edge_out)
    edge_out[0, 0:1, :rows] = image.T[cols - 1 : cols, :]
    edge_out[1, 0:1, :rows] = image.T[0:1, :]
    edge_out[2, 0:1, :cols] = image[rows - 1 : rows, :]
    edge_out[3, 0:1, :cols] = image[0:1, :]

    def turn(origin, into, base, axis):
        width = lines[2 * axis]
        group = LANES // width

        def some(index, carry):
            first = index * group
            block = []
            for h in range(halves):
                if axis == 0:
                    parts = [
                        origin[h, pl.ds(first + j, width, stride=cols), :] for j in range(group)
                    ]
                    block.append(jnp.concatenate(parts, axis=0))
                else:
                    at = pl.ds(index * LANES, LANES)
                    block.append(origin[h, at, :])
            block = jnp.concatenate(block, axis=1).astype(jnp.float32).astype(jnp.bfloat16)
            def product(part):
                return lax.dot_general(
                    order[...], part, (((1,), (1,)), ((), ())), preferred_element_type=jnp.float32
                )

            whole = product(block)
            for j in range(group):
                if j >= group - DIRECT:
                    alone = product(block[j * width : (j + 1) * width])
                    into[base + first + j, :, :, :width] = alone.reshape(nv, SUBLANES, width)
                else:
                    moved = pltpu.roll(whole, LANES - j * width, 1) if j else whole
                    into[base + first + j] = moved.reshape(nv, SUBLANES, LANES)
            return carry

        for index in range(rows * cols // LANES):
            some(index, None)

    def turn_across(origin, base):
        turn(origin, across_costs, base, 0)

    def turn_down(origin, base):
        turn(origin, down_costs, base, 1)

    def take_mate():
        for _, copy in mate_copies:
            copy.wait_recv()
        at = pl.ds(pl.multiple_of(cols - own_base, SUBLANES), cols)
        image_lines[0, at, :rows] = mate_image[...].T
        turn_across(mate_raw, spans[0] + cols)

    pl.semaphore_wait(barrier, awaited)
    start(mate_copies[:1])
    for k in range(4):
        start(edge_copies[k])
    for copy in locals_[3:]:
        copy.wait()
    start(mate_copies[1:])

    def start_far():
        for k in range(4):
            start(far_raw_copies[k])

    pl.when(core == 0)(start_far)

    shape = (disparities, disparities)
    source = lax.broadcasted_iota(jnp.int32, shape, 1)
    target = lax.broadcasted_iota(jnp.int32, shape, 0)
    wanted = target // SUBLANES + nv * (target % SUBLANES)
    order[...] = jnp.where(source == wanted, 1.0, 0.0).astype(jnp.bfloat16)


    pl.when(iz < nz - 1)(lambda: turn_down(own_raw, rows))
    turn_across(own_raw, spans[0])
    pl.when(iz == nz - 1)(take_mate)

    sub = lax.broadcasted_iota(jnp.int32, (SUBLANES, LANES), 0)
    lane = lax.broadcasted_iota(jnp.int32, (SUBLANES, LANES), 1)

    def penalties(k):
        axis = k // 2
        small = small_ref[k].astype(jnp.float32)
        large = large_ref[k].astype(jnp.float32)
        span = spans[axis]
        own = image_lines[axis, :span, :]
        edge = edge_in[k, 0:1, :]
        if backward[k]:
            before = jnp.concatenate([own[1:], edge], axis=0)
        else:
            before = jnp.concatenate([edge, own[:-1]], axis=0)
        large_lines[k, span : 2 * span] = small + (large - small) / (
            1.0 + GRADIENT_GAIN * jnp.abs(own - before)
        )

    def early_penalties(k):
        edge_in[k] = jnp.zeros((SUBLANES, LANES), jnp.float32)
        penalties(k)
        start(far_large_copies[k])

    def later_penalties(k):
        edge_copies[k][0][1].wait_recv()
        penalties(k)
        start(far_large_copies[k])

    def task(k):
        axis = k // 2
        length, width = lengths[k], lines[k]
        group = LANES // width
        small = small_ref[k].astype(jnp.float32)
        step_costs = costs[axis]
        span = spans[axis]
        first = place[k] == 0
        pl.when(first)(lambda: early_penalties(k))
        ends = both(is_last[k], jnp.logical_not(first)) if SKIPS[k] else False
        receives = jnp.logical_not(first)
        if SKIPS[k]:
            pl.when(ends)(far_large_copies[k][0][1].wait_recv)
            receives = jnp.where(is_last[k], place[k] > 1, receives)

        @pl.when(receives)
        def _():
            path_copies[k][0][1].wait_recv()

        @pl.when(jnp.logical_not(receives))
        def _():
            inbox[k] = jnp.zeros(inbox.shape[1:], jnp.float32)

        for v in range(nv):
            packed = inbox[k, v // group]
            shift = (v % group) * width
            paths[k, 0, v] = pltpu.roll(packed, LANES - shift, 1) if shift else packed

        def load(at):
            return [paths[k, at, v] for v in range(nv)]

        def store(at, state):
            for v in range(nv):
                paths[k, at, v] = state[v]

        def step(line, cost_line, state):
            capped = large_lines[k, pl.ds(line, SUBLANES, stride=0), :]
            under = jnp.where(sub == 0, FAR, pltpu.roll(state[-1], 1, 0))
            over = jnp.where(sub == SUBLANES - 1, FAR, pltpu.roll(state[0], SUBLANES - 1, 0))
            beside = []
            for v in range(nv):
                low = state[v - 1] if v else under
                high = state[v + 1] if v < nv - 1 else over
                beside.append(jnp.minimum(low, high))
            if nv % 4 == 0:
                lowest = tree_min([beside[v] for v in range(nv) if v % 4 in (1, 2)])
            else:
                lowest = tree_min(state)
            lowest = all_sublanes_min(lowest)
            capped = capped + lowest
            fresh = []
            for v in range(nv):
                near = jnp.minimum(state[v], beside[v] + small)
                fresh.append(step_costs[cost_line, v] + jnp.minimum(near, capped))
            return fresh, lowest

        def early(index, carry):
            state = load(0)
            for part in range(UNROLL):
                at = index * UNROLL + part
                if backward[k]:
                    at = jnp.where(at < span, span - 1 - at, 3 * span - 1 - at)
                cost_at = at
                if axis == 0:
                    cost_at = jnp.where(at < span, at, at + own_base)
                state, _ = step(at, cost_at, state)
            store(0, state)
            return carry

        def late(index, carry):
            state = load(index * UNROLL)
            for part in range(UNROLL):
                at = index * UNROLL + part
                line = length - 1 - at if backward[k] else at
                own_line = span + (own_base if axis == 0 else 0) + line
                state, lowest = step(own_line, span + line, state)
                store(at + 1, state)
                lowests[k, at] = lowest
            return carry

        begin = jnp.where(ends, 0, span // UNROLL) if SKIPS[k] else span // UNROLL
        end = span // UNROLL
        if axis == 0:
            end = jnp.where(hands_on[k], (span + length) // UNROLL, end)
        lax.fori_loop(begin, end, early, 0)
        lax.fori_loop(0, length // UNROLL, late, 0)

        after = places[k] - 1 - place[k]

        @pl.when(both(hands_on[k], after >= (2 if SKIPS[k] else 1)))
        def _():
            above = lowests[k, length - 1]
            sent = [part - above for part in load(length)]
            for slot in range(nv // group):
                packed = sent[slot * group]
                for g in range(1, group):
                    moved = pltpu.roll(sent[slot * group + g], g * width, 1)
                    packed = jnp.where(lane >= g * width, moved, packed)
                outbox[k, slot] = packed

        start(path_copies[k])

    def total(axis):
        k = 2 * axis
        width = lines[k]
        group = LANES // width

        def some(index):
            for j in range(group):
                line = index * group + j
                back = lengths[k] - 1 - line
                above = lowests[k, line] + lowests[k + 1, back]
                parts = [above] + [
                    paths[k, line + 1, v] + paths[k + 1, back + 1, v] for v in range(nv)
                ]
                if j:
                    parts = [
                        jnp.where(lane >= j * width, pltpu.roll(part, j * width, 1), before)
                        for part, before in zip(parts, packed)
                    ]
                packed = parts
            packed = [part - packed[0] for part in packed[1:]]
            for v in range(nv):
                turned[index, pl.ds(v, SUBLANES, stride=nv), :] = packed[v]
            for h in range(halves):
                block = turned[index, h * LANES : (h + 1) * LANES].T
                if axis == 0:
                    for j in range(group):
                        at = pl.ds(index * group + j, width, stride=cols)
                        totals[axis, h, at, :] = block[j * width : (j + 1) * width]
                else:
                    totals[axis, h, pl.ds(index * LANES, LANES), :] = block

        for index in range(rows * cols // LANES):
            some(index)

    turns = max(nz, ny)
    turn_down_at = [
        jnp.where(places[k] - 1 - place[k] == 1, place[k] + 1, place[k]) if SKIPS[k] else place[k]
        for k in (2, 3)
    ]
    down_done = jnp.maximum(*turn_down_at)
    turn_left = jnp.where(places[1] - 1 - place[1] >= 2, place[1], turns)
    ends_left = both(is_last[1], place[1] > 0)

    def take_forward():
        forward_copies[1][0][1].wait_recv()
        turn_across(far_across.at[1 - core], cols - own_base)

    def one_turn(turn_at, carry):
        pl.when(both(turn_at == turns, ends_left, core == 0))(take_forward)
        pl.when(turn_at == turn_left)(lambda: task(1))
        pl.when(both(turn_at == 0, iz == nz - 1))(lambda: turn_down(own_raw, rows))
        pl.when(turn_at == turn_down_at[0])(lambda: task(2))
        pl.when(turn_at == turn_down_at[1])(lambda: task(3))
        pl.when(both(turn_at == 0, iz < nz - 1))(take_mate)
        pl.when(both(turn_at == 0, core != 0))(start_far)

        pl.when(turn_at == down_done)(lambda: total(1))
        pl.when(turn_at == place[0])(lambda: task(0))

        @pl.when(turn_at == 0)
        def _():
            for k in range(4):
                pl.when(place[k] > 0)(functools.partial(later_penalties, k))

        fetched = turn_at == max(turns - 3, 0)

        pl.when(both(fetched, ends_left, core != 0))(take_forward)

        @pl.when(both(fetched, ends_left))
        def _():
            far_raw_copies[1][0][1].wait_recv()
            start(forward_copies[1])
            turn_across(far_across.at[core], own_base)

        for k in (2, 3):

            @pl.when(both(fetched, is_last[k], place[k] > 0))
            def _(k=k):
                far_raw_copies[k][0][1].wait_recv()
                turn_down(far_raw, 0)

        return carry

    lax.fori_loop(0, turns + 1, one_turn, 0)
    total(0)
    for h in range(halves):
        out_ref[:, h * LANES : (h + 1) * LANES] = (totals[0, h] + totals[1, h]) * OUT_SCALE

    drain(mate_copies)
    pl.when(ends_left)(forward_copies[1][0][1].wait_send)
    for k in range(4):
        drain(edge_copies[k])
        drain(path_copies[k])
        drain(far_raw_copies[k])
        drain(far_large_copies[k])


def on_device(cost_volume, left_image, p_small, p_large):
    rows, cols, disparities = cost_volume.shape
    nv = disparities // SUBLANES
    longest = max(rows, cols)
    packed = nv * longest // LANES
    halves = disparities // LANES
    block = (halves, rows * cols, LANES)
    hbm = pl.BlockSpec(memory_space=pltpu.HBM)
    vmem = pl.BlockSpec(memory_space=pltpu.VMEM)
    total = pl.pallas_call(
        functools.partial(kernel, rows, cols),
        out_shape=jax.ShapeDtypeStruct((rows * cols, disparities), jnp.float32),
        in_specs=[hbm] * 4,
        out_specs=vmem,
        scratch_shapes=[
            pltpu.SMEM((4,), jnp.int32),
            pltpu.SMEM((4,), jnp.int32),
            pltpu.VMEM((rows, cols), jnp.float32),
            pltpu.VMEM((rows, cols), jnp.float32),
            pltpu.VMEM(block, jnp.int32),
            pltpu.VMEM(block, jnp.int32),
            pltpu.VMEM(block, jnp.int32),
            pltpu.VMEM((CORES, *block), jnp.int32),
            pltpu.VMEM((rows * cols // LANES, disparities, LANES), jnp.float32),
            pltpu.VMEM((disparities, disparities), jnp.bfloat16),
            pltpu.VMEM((2, halves, rows * cols, LANES), jnp.float32),
            pltpu.VMEM((2 * CORES * cols, nv, SUBLANES, LANES), jnp.float32),
            pltpu.VMEM((2 * rows, nv, SUBLANES, LANES), jnp.float32),
            pltpu.VMEM((4, longest + 1, nv, SUBLANES, LANES), jnp.float32),
            pltpu.VMEM((4, longest, SUBLANES, LANES), jnp.float32),
            pltpu.VMEM((4, 2 * CORES * longest, LANES), jnp.float32),
            pltpu.VMEM((2, CORES * longest, LANES), jnp.float32),
            pltpu.VMEM((4, packed, SUBLANES, LANES), jnp.float32),
            pltpu.VMEM((4, packed, SUBLANES, LANES), jnp.float32),
            pltpu.VMEM((4, SUBLANES, LANES), jnp.float32),
            pltpu.VMEM((4, SUBLANES, LANES), jnp.float32),
            pltpu.SemaphoreType.DMA((SENDS,)),
            pltpu.SemaphoreType.DMA((20,)),
            pltpu.SemaphoreType.DMA((3 + halves,)),
        ],
        compiler_params=pltpu.CompilerParams(
            collective_id=0,
            has_side_effects=True,
            vmem_limit_bytes=VMEM_BYTES,
        ),
    )(
        *(
            pltpu.with_memory_space_constraint(array, pltpu.HBM)
            for array in (
                cost_volume.reshape(rows * cols, disparities),
                left_image,
                p_small,
                p_large,
            )
        )
    )
    return total.reshape(rows, cols, disparities)


def solution(mesh):
    in_specs = (P("gy", "gx", None), P("gy", "gx"), P(), P())
    out_specs = P("gy", "gx", None)
    return jax.shard_map(
        on_device, mesh=mesh, in_specs=in_specs, out_specs=out_specs, check_vma=False
    )
```

```python
import functools

import jax
import jax.numpy as jnp
from jax import lax
from jax.experimental import pallas as pl
from jax.experimental.pallas import tpu as pltpu
from jax.sharding import PartitionSpec as P

FAR = 1e30
GRADIENT_GAIN = 4.0
OUT_SCALE = 1.0 / 256.0
LANES = 128
SUBLANES = 8
UNROLL = 2
CORES = 2
DIRECT = 3
SENDS = 30
VMEM_BYTES = 40 << 20
SKIPS = (False, True, True, True)
MESH = pl.DeviceIdType.MESH


def tree_min(parts):
    parts = list(parts)
    while len(parts) > 1:
        pairs = [jnp.minimum(a, b) for a, b in zip(parts[::2], parts[1::2])]
        parts = pairs + ([parts[-1]] if len(parts) % 2 else [])
    return parts[0]


def all_sublanes_min(x):
    for by in (4, 2, 1):
        x = jnp.minimum(x, pltpu.roll(x, by, 0))
    return x


def kernel(
    rows,
    cols,
    cost_hbm,
    image_hbm,
    small_hbm,
    large_hbm,
    out_ref,
    small_ref,
    large_ref,
    own_image,
    mate_image,
    own_raw,
    mate_raw,
    far_raw,
    far_across,
    turned,
    order,
    totals,
    across_costs,
    down_costs,
    paths,
    lowests,
    large_lines,
    image_lines,
    outbox,
    inbox,
    edge_out,
    edge_in,
    send_sems,
    recv_sems,
    local_sems,
):
    disparities = cost_hbm.shape[1]
    nv = disparities // SUBLANES
    halves = disparities // LANES
    nx, ny = lax.axis_size("gx"), lax.axis_size("gy")
    ix, iy = lax.axis_index("gx"), lax.axis_index("gy")
    nz = nx // CORES
    iz, core = ix // CORES, ix % CORES
    mate = {"gx": iz * CORES + 1 - core}
    own_base = core * cols
    spans = (CORES * cols, rows)
    costs = (across_costs, down_costs)
    lengths = (cols, cols, rows, rows)
    lines = (rows, rows, cols, cols)
    backward = (False, True, False, True)

    place = (iz, nz - 1 - iz, iy, ny - 1 - iy)
    places = (nz, nz, ny, ny)
    hands_on = (core == 1, core == 0, True, True)
    is_last = [place[k] == places[k] - 1 for k in range(4)]

    def next_across(k, by, to_core):
        step = -by if backward[k] else by
        return {"gx": (iz + step) * CORES + to_core}

    def next_down(k, by):
        return {"gy": iy - by if backward[k] else iy + by}

    def prev_across(k, by):
        return next_across(k, -by, 0 if backward[k] else 1)

    def both(*flags):
        result = True
        for flag in flags:
            result = flag if result is True else jnp.logical_and(result, flag)
        return result

    sends = iter(range(SENDS))

    def remote(source, target, recv, device):
        return pltpu.make_async_remote_copy(
            src_ref=source,
            dst_ref=target,
            send_sem=send_sems.at[next(sends)],
            recv_sem=recv_sems.at[recv],
            device_id=device,
            device_id_type=MESH,
        )

    mate_copies = [
        (None, remote(own_image, mate_image, 0, mate)),
        (None, remote(own_raw, mate_raw, 1, mate)),
    ]
    edge_copies, path_copies, far_raw_copies, far_large_copies = [], [], [], []
    forward_copies = {}
    for k in range(4):
        sent = hands_on[k]
        after = places[k] - 1 - place[k]
        near_end = 2 if SKIPS[k] else 1
        if k < 2:
            to = lambda by, k=k: [
                next_across(k, by, c) for c in ((0, 1) if backward[k] else (1, 0))
            ]
            same_core = next_across(k, 1, core)
        else:
            to = lambda by, k=k: [next_down(k, by)]
            same_core = next_down(k, 1)
        edge_copies.append(
            [
                (both(sent, after >= 1), remote(edge_out.at[k], edge_in.at[k], 2 + k, device))
                for device in to(1)
            ]
        )
        path_copies.append(
            [
                (both(sent, after >= near_end), remote(outbox.at[k], inbox.at[k], 6 + k, device))
                for device in to(1)
            ]
        )
        if SKIPS[k]:
            path_copies[k] = [
                (both(sent, after == 2), remote(outbox.at[k], inbox.at[k], 6 + k, device))
                for device in to(2)
            ] + path_copies[k]
            span = spans[k // 2]
            target = far_across.at[core] if k < 2 else far_raw
            far_raw_copies.append([(after == 1, remote(own_raw, target, 10 + k, same_core))])
            far_large_copies.append(
                [
                    (
                        after == 1,
                        remote(
                            large_lines.at[k, pl.ds(span, span)],
                            large_lines.at[k, pl.ds(0, span)],
                            14 + k,
                            same_core,
                        ),
                    )
                ]
            )
            if k < 2:
                here = far_across.at[core]
                forward_copies[k] = [(None, remote(here, here, 18 + k, mate))]
        else:
            far_raw_copies.append([])
            far_large_copies.append([])

    def start(copies):
        for flag, copy in copies:
            if flag is None:
                copy.start()
            else:
                pl.when(flag)(copy.start)

    def drain(copies):
        for flag, copy in copies:
            if flag is None:
                copy.wait_send()
            else:
                pl.when(flag)(copy.wait_send)

    locals_ = [
        pltpu.make_async_copy(source, target, local_sems.at[at])
        for at, (source, target) in enumerate(
            (
                (image_hbm, own_image),
                (small_hbm, small_ref),
                (large_hbm, large_ref),
                *(
                    (cost_hbm.at[:, pl.ds(h * LANES, LANES)], own_raw.at[h])
                    for h in range(halves)
                ),
            )
        )
    ]
    for copy in locals_:
        copy.start()

    barrier = pltpu.get_barrier_semaphore()

    def greet(device):
        pl.semaphore_signal(barrier, inc=1, device_id=device, device_id_type=MESH)

    greet(mate)
    awaited = jnp.int32(1)
    for k in range(4):
        after = places[k] - 1 - place[k]
        ends = both(after == 0, place[k] > 0)
        skips = both(after == 0, place[k] > 1)
        if k < 2:
            pl.when(place[k] > 0)(functools.partial(greet, prev_across(k, 1)))
            awaited += jnp.where(both(hands_on[k], after >= 1), CORES, 0)
            if SKIPS[k]:
                far_only = jnp.logical_not(hands_on[k])
                pl.when(both(ends, far_only))(
                    functools.partial(greet, next_across(k, -1, core))
                )
                awaited += jnp.where(both(far_only, after == 1), 1, 0)
                pl.when(skips)(functools.partial(greet, prev_across(k, 2)))
                awaited += jnp.where(both(hands_on[k], after == 2), CORES, 0)
        else:
            pl.when(place[k] > 0)(functools.partial(greet, next_down(k, -1)))
            awaited += jnp.where(after >= 1, 1, 0)
            if SKIPS[k]:
                pl.when(skips)(functools.partial(greet, next_down(k, -2)))
                awaited += jnp.where(after == 2, 1, 0)

    for copy in locals_[:3]:
        copy.wait()
    image = own_image[...]
    image_lines[...] = jnp.zeros_like(image_lines)
    image_lines[1, 0:rows, :cols] = image
    image_lines[0, pl.ds(pl.multiple_of(own_base, SUBLANES), cols), :rows] = image.T
    edge_out[...] = jnp.zeros_like(edge_out)
    edge_out[0, 0:1, :rows] = image.T[cols - 1 : cols, :]
    edge_out[1, 0:1, :rows] = image.T[0:1, :]
    edge_out[2, 0:1, :cols] = image[rows - 1 : rows, :]
    edge_out[3, 0:1, :cols] = image[0:1, :]

    def turn(origin, into, base, axis):
        width = lines[2 * axis]
        group = LANES // width

        def some(index, carry):
            first = index * group
            block = []
            for h in range(halves):
                if axis == 0:
                    parts = [
                        origin[h, pl.ds(first + j, width, stride=cols), :] for j in range(group)
                    ]
                    block.append(jnp.concatenate(parts, axis=0))
                else:
                    at = pl.ds(index * LANES, LANES)
                    block.append(origin[h, at, :])
            block = jnp.concatenate(block, axis=1).astype(jnp.float32).astype(jnp.bfloat16)
            def product(part):
                return lax.dot_general(
                    order[...], part, (((1,), (1,)), ((), ())), preferred_element_type=jnp.float32
                )

            whole = product(block)
            for j in range(group):
                if j >= group - DIRECT:
                    alone = product(block[j * width : (j + 1) * width])
                    into[base + first + j, :, :, :width] = alone.reshape(nv, SUBLANES, width)
                else:
                    moved = pltpu.roll(whole, LANES - j * width, 1) if j else whole
                    into[base + first + j] = moved.reshape(nv, SUBLANES, LANES)
            return carry

        for index in range(rows * cols // LANES):
            some(index, None)

    def turn_across(origin, base):
        turn(origin, across_costs, base, 0)

    def turn_down(origin, base):
        turn(origin, down_costs, base, 1)

    def take_mate():
        for _, copy in mate_copies:
            copy.wait_recv()
        at = pl.ds(pl.multiple_of(cols - own_base, SUBLANES), cols)
        image_lines[0, at, :rows] = mate_image[...].T
        turn_across(mate_raw, spans[0] + cols)

    pl.semaphore_wait(barrier, awaited)
    start(mate_copies[:1])
    for k in range(4):
        start(edge_copies[k])
    for copy in locals_[3:]:
        copy.wait()

    def start_far():
        for k in range(4):
            start(far_raw_copies[k])

    at_start = iz == nz - 1
    pl.when(at_start)(mate_copies[1][1].start)
    pl.when(core == 0)(start_far)
    pl.when(jnp.logical_not(at_start))(mate_copies[1][1].start)

    shape = (disparities, disparities)
    source = lax.broadcasted_iota(jnp.int32, shape, 1)
    target = lax.broadcasted_iota(jnp.int32, shape, 0)
    wanted = target // SUBLANES + nv * (target % SUBLANES)
    order[...] = jnp.where(source == wanted, 1.0, 0.0).astype(jnp.bfloat16)


    pl.when(iz < nz - 1)(lambda: turn_down(own_raw, rows))
    turn_across(own_raw, spans[0])
    pl.when(iz == nz - 1)(take_mate)

    sub = lax.broadcasted_iota(jnp.int32, (SUBLANES, LANES), 0)
    lane = lax.broadcasted_iota(jnp.int32, (SUBLANES, LANES), 1)

    def penalties(k):
        axis = k // 2
        small = small_ref[k].astype(jnp.float32)
        large = large_ref[k].astype(jnp.float32)
        span = spans[axis]
        own = image_lines[axis, :span, :]
        edge = edge_in[k, 0:1, :]
        if backward[k]:
            before = jnp.concatenate([own[1:], edge], axis=0)
        else:
            before = jnp.concatenate([edge, own[:-1]], axis=0)
        large_lines[k, span : 2 * span] = small + (large - small) / (
            1.0 + GRADIENT_GAIN * jnp.abs(own - before)
        )

    def early_penalties(k):
        edge_in[k] = jnp.zeros((SUBLANES, LANES), jnp.float32)
        penalties(k)
        start(far_large_copies[k])

    def later_penalties(k):
        edge_copies[k][0][1].wait_recv()
        penalties(k)
        start(far_large_copies[k])

    def task(k):
        axis = k // 2
        length, width = lengths[k], lines[k]
        group = LANES // width
        small = small_ref[k].astype(jnp.float32)
        step_costs = costs[axis]
        span = spans[axis]
        first = place[k] == 0
        pl.when(first)(lambda: early_penalties(k))
        ends = both(is_last[k], jnp.logical_not(first)) if SKIPS[k] else False
        receives = jnp.logical_not(first)
        if SKIPS[k]:
            pl.when(ends)(far_large_copies[k][0][1].wait_recv)
            receives = jnp.where(is_last[k], place[k] > 1, receives)

        @pl.when(receives)
        def _():
            path_copies[k][0][1].wait_recv()

        @pl.when(jnp.logical_not(receives))
        def _():
            inbox[k] = jnp.zeros(inbox.shape[1:], jnp.float32)

        for v in range(nv):
            packed = inbox[k, v // group]
            shift = (v % group) * width
            paths[k, 0, v] = pltpu.roll(packed, LANES - shift, 1) if shift else packed

        def load(at):
            return [paths[k, at, v] for v in range(nv)]

        def store(at, state):
            for v in range(nv):
                paths[k, at, v] = state[v]

        def step(line, cost_line, state):
            capped = large_lines[k, pl.ds(line, SUBLANES, stride=0), :]
            under = jnp.where(sub == 0, FAR, pltpu.roll(state[-1], 1, 0))
            over = jnp.where(sub == SUBLANES - 1, FAR, pltpu.roll(state[0], SUBLANES - 1, 0))
            beside = []
            for v in range(nv):
                low = state[v - 1] if v else under
                high = state[v + 1] if v < nv - 1 else over
                beside.append(jnp.minimum(low, high))
            if nv % 4 == 0:
                lowest = tree_min([beside[v] for v in range(nv) if v % 4 in (1, 2)])
            else:
                lowest = tree_min(state)
            lowest = all_sublanes_min(lowest)
            capped = capped + lowest
            fresh = []
            for v in range(nv):
                near = jnp.minimum(state[v], beside[v] + small)
                fresh.append(step_costs[cost_line, v] + jnp.minimum(near, capped))
            return fresh, lowest

        def early(index, carry):
            state = load(0)
            for part in range(UNROLL):
                at = index * UNROLL + part
                if backward[k]:
                    at = jnp.where(at < span, span - 1 - at, 3 * span - 1 - at)
                cost_at = at
                if axis == 0:
                    cost_at = jnp.where(at < span, at, at + own_base)
                state, _ = step(at, cost_at, state)
            store(0, state)
            return carry

        def late(index, carry):
            state = load(index * UNROLL)
            for part in range(UNROLL):
                at = index * UNROLL + part
                line = length - 1 - at if backward[k] else at
                own_line = span + (own_base if axis == 0 else 0) + line
                state, lowest = step(own_line, span + line, state)
                store(at + 1, state)
                lowests[k, at] = lowest
            return carry

        begin = jnp.where(ends, 0, span // UNROLL) if SKIPS[k] else span // UNROLL
        end = span // UNROLL
        if axis == 0:
            end = jnp.where(hands_on[k], (span + length) // UNROLL, end)
        lax.fori_loop(begin, end, early, 0)
        lax.fori_loop(0, length // UNROLL, late, 0)

        after = places[k] - 1 - place[k]

        @pl.when(both(hands_on[k], after >= (2 if SKIPS[k] else 1)))
        def _():
            above = lowests[k, length - 1]
            sent = [part - above for part in load(length)]
            for slot in range(nv // group):
                packed = sent[slot * group]
                for g in range(1, group):
                    moved = pltpu.roll(sent[slot * group + g], g * width, 1)
                    packed = jnp.where(lane >= g * width, moved, packed)
                outbox[k, slot] = packed

        start(path_copies[k])

    def total(axis):
        k = 2 * axis
        width = lines[k]
        group = LANES // width

        def some(index):
            for j in range(group):
                line = index * group + j
                back = lengths[k] - 1 - line
                above = lowests[k, line] + lowests[k + 1, back]
                parts = [above] + [
                    paths[k, line + 1, v] + paths[k + 1, back + 1, v] for v in range(nv)
                ]
                if j:
                    parts = [
                        jnp.where(lane >= j * width, pltpu.roll(part, j * width, 1), before)
                        for part, before in zip(parts, packed)
                    ]
                packed = parts
            packed = [part - packed[0] for part in packed[1:]]
            for v in range(nv):
                turned[index, pl.ds(v, SUBLANES, stride=nv), :] = packed[v]
            for h in range(halves):
                block = turned[index, h * LANES : (h + 1) * LANES].T
                if axis == 0:
                    for j in range(group):
                        at = pl.ds(index * group + j, width, stride=cols)
                        totals[axis, h, at, :] = block[j * width : (j + 1) * width]
                else:
                    totals[axis, h, pl.ds(index * LANES, LANES), :] = block

        for index in range(rows * cols // LANES):
            some(index)

    turns = max(nz, ny)
    turn_down_at = [
        jnp.where(places[k] - 1 - place[k] == 1, place[k] + 1, place[k]) if SKIPS[k] else place[k]
        for k in (2, 3)
    ]
    down_done = jnp.maximum(*turn_down_at)
    turn_left = jnp.where(places[1] - 1 - place[1] >= 2, place[1], turns)
    ends_left = both(is_last[1], place[1] > 0)

    def take_forward():
        forward_copies[1][0][1].wait_recv()
        turn_across(far_across.at[1 - core], cols - own_base)

    def one_turn(turn_at, carry):
        pl.when(both(turn_at == turns, ends_left, core == 0))(take_forward)
        pl.when(turn_at == turn_left)(lambda: task(1))
        pl.when(both(turn_at == 0, iz == nz - 1))(lambda: turn_down(own_raw, rows))
        pl.when(turn_at == turn_down_at[0])(lambda: task(2))
        pl.when(turn_at == turn_down_at[1])(lambda: task(3))
        pl.when(both(turn_at == 0, iz < nz - 1))(take_mate)
        pl.when(both(turn_at == 0, core != 0))(start_far)

        pl.when(turn_at == down_done)(lambda: total(1))
        pl.when(turn_at == place[0])(lambda: task(0))

        @pl.when(turn_at == 0)
        def _():
            for k in range(4):
                pl.when(place[k] > 0)(functools.partial(later_penalties, k))

        fetched = turn_at == max(turns - 3, 0)

        pl.when(both(fetched, ends_left, core != 0))(take_forward)

        @pl.when(both(fetched, ends_left))
        def _():
            far_raw_copies[1][0][1].wait_recv()
            start(forward_copies[1])
            turn_across(far_across.at[core], own_base)

        for k in (2, 3):

            @pl.when(both(fetched, is_last[k], place[k] > 0))
            def _(k=k):
                far_raw_copies[k][0][1].wait_recv()
                turn_down(far_raw, 0)

        return carry

    lax.fori_loop(0, turns + 1, one_turn, 0)
    total(0)
    for h in range(halves):
        out_ref[:, h * LANES : (h + 1) * LANES] = (totals[0, h] + totals[1, h]) * OUT_SCALE

    drain(mate_copies)
    pl.when(ends_left)(forward_copies[1][0][1].wait_send)
    for k in range(4):
        drain(edge_copies[k])
        drain(path_copies[k])
        drain(far_raw_copies[k])
        drain(far_large_copies[k])


def on_device(cost_volume, left_image, p_small, p_large):
    rows, cols, disparities = cost_volume.shape
    nv = disparities // SUBLANES
    longest = max(rows, cols)
    packed = nv * longest // LANES
    halves = disparities // LANES
    block = (halves, rows * cols, LANES)
    hbm = pl.BlockSpec(memory_space=pltpu.HBM)
    vmem = pl.BlockSpec(memory_space=pltpu.VMEM)
    total = pl.pallas_call(
        functools.partial(kernel, rows, cols),
        out_shape=jax.ShapeDtypeStruct((rows * cols, disparities), jnp.float32),
        in_specs=[hbm] * 4,
        out_specs=vmem,
        scratch_shapes=[
            pltpu.SMEM((4,), jnp.int32),
            pltpu.SMEM((4,), jnp.int32),
            pltpu.VMEM((rows, cols), jnp.float32),
            pltpu.VMEM((rows, cols), jnp.float32),
            pltpu.VMEM(block, jnp.int32),
            pltpu.VMEM(block, jnp.int32),
            pltpu.VMEM(block, jnp.int32),
            pltpu.VMEM((CORES, *block), jnp.int32),
            pltpu.VMEM((rows * cols // LANES, disparities, LANES), jnp.float32),
            pltpu.VMEM((disparities, disparities), jnp.bfloat16),
            pltpu.VMEM((2, halves, rows * cols, LANES), jnp.float32),
            pltpu.VMEM((2 * CORES * cols, nv, SUBLANES, LANES), jnp.float32),
            pltpu.VMEM((2 * rows, nv, SUBLANES, LANES), jnp.float32),
            pltpu.VMEM((4, longest + 1, nv, SUBLANES, LANES), jnp.float32),
            pltpu.VMEM((4, longest, SUBLANES, LANES), jnp.float32),
            pltpu.VMEM((4, 2 * CORES * longest, LANES), jnp.float32),
            pltpu.VMEM((2, CORES * longest, LANES), jnp.float32),
            pltpu.VMEM((4, packed, SUBLANES, LANES), jnp.float32),
            pltpu.VMEM((4, packed, SUBLANES, LANES), jnp.float32),
            pltpu.VMEM((4, SUBLANES, LANES), jnp.float32),
            pltpu.VMEM((4, SUBLANES, LANES), jnp.float32),
            pltpu.SemaphoreType.DMA((SENDS,)),
            pltpu.SemaphoreType.DMA((20,)),
            pltpu.SemaphoreType.DMA((3 + halves,)),
        ],
        compiler_params=pltpu.CompilerParams(
            collective_id=0,
            has_side_effects=True,
            vmem_limit_bytes=VMEM_BYTES,
        ),
    )(
        *(
            pltpu.with_memory_space_constraint(array, pltpu.HBM)
            for array in (
                cost_volume.reshape(rows * cols, disparities),
                left_image,
                p_small,
                p_large,
            )
        )
    )
    return total.reshape(rows, cols, disparities)


def solution(mesh):
    in_specs = (P("gy", "gx", None), P("gy", "gx"), P(), P())
    out_specs = P("gy", "gx", None)
    return jax.shard_map(
        on_device, mesh=mesh, in_specs=in_specs, out_specs=out_specs, check_vma=False
    )
```
